32 devices in a mesh: lon: 8 (over z, y), lat: 4 (over x, core).
Axes of the slice: x: 2, y: 2, z: 4, core: 2. Of those that a mesh axis runs over, the one named last changes fastest.
Arguments:
- tracer: float32 [4, 8, 128, 2048], P(None, None, 'lat', 'lon'), may hold values from -6 to 6
- velocity: float32 [2, 8, 128, 2048], P(None, None, 'lat', 'lon'), may hold values from -2 to 2
- land_mask: int32 [128, 2048], P('lat', 'lon'), may hold values 0 or 1
- fold_map: int32 [2048], P('lon'), may hold values from 0 to 2047, as said below
- nested_tracer_field: float32 [4, 8, 4, 16384], P(None, None, 'lat', 'lon'), may hold values from -6 to 6
- nested_cell_volume: float32 [4, 16384], P('lat', 'lon'), may hold values from 0.05 to 0.2
- nest_parent: int32 [4, 16384], P('lat', 'lon'), may hold values from -1 to 65535, as said below
Outputs:
- tracer_next: float32 [4, 8, 128, 2048], P(None, None, 'lat', 'lon')
The draws below stay inside these ranges and needn't reach their ends.
Inputs may be any that keep to these rules, and one draw needn't show every extreme that they name: fold_map pairs the columns of longitude block j (columns j * 256 to j * 256 + 255) one to one with those of block 7 - j, and fold_map[fold_map[i]] = i. `nest_parent`: A slot's parent p lies in longitude block p // 8192. Of the 2048 slots of one device (one row, one longitude block of slots) at most 512 name parents in any one longitude block; in every row one longitude block receives exactly 512 from every device of the row; some slot names the last cell of the last longitude block.
All inputs are finite; a program needn't handle non-finite values. No bound on the sum of `land_mask` on one device may be relied on, other than what follows from the above.
Results may differ from the reference program's by a relative error of at most 0.000041.
Values sent between devices are 32-bit elements; how exact they have to be, the bound alone decides.
No kernel may reach another device: no remote copies, remote signals or barrier semaphores. Data moves between devices by JAX's collectives and lax.ppermute only.
A program may use at most 128 MiB of HBM per device.

```python
import math
import jax
import jax.numpy as jnp
from jax import lax

TRACER_TOTAL = 4
DEPTH_LEVELS = 8
CLAT = 32
CLON = 256
NEST_DEV = 2048
NLAT = 128
NLON = 2048
NEST_SLOT_ROWS = 4
SLOTS_PER_ROW = 16384


def draw_fold_map(key, part):
    block_count = NLON // CLON
    half_count = block_count // 2
    keys = jax.random.split(jax.random.fold_in(key, 11), half_count)
    forward = jax.vmap(lambda single: jax.random.permutation(single, CLON))(keys).astype(jnp.int32)
    backward = jnp.argsort(forward, axis=1, stable=True).astype(jnp.int32)
    offsets = jnp.concatenate([forward, backward[::-1]], axis=0)
    bases = (block_count - 1 - jnp.arange(block_count, dtype=jnp.int32)) * CLON
    return (bases[:, None] + offsets).reshape(-1).astype(jnp.int32)


def draw_nest_parent(key, part):
    row_count = NLAT // CLAT
    block_count = NLON // CLON
    bound = 2 * NEST_DEV // block_count
    block_cells = CLAT * CLON
    shape = (row_count, block_count, NEST_DEV)
    heavy = jax.random.randint(jax.random.fold_in(key, 21), (row_count, 1, 1), 0, block_count).astype(jnp.int32)
    rotate = jax.random.randint(jax.random.fold_in(key, 22), (row_count, block_count, 1), 0, block_count - 1).astype(jnp.int32)
    forced = (block_count - 2 - heavy[:, 0, :]) % block_count % (block_count - 1)
    rotate = rotate.at[:, 0, :].set(forced.astype(jnp.int32))
    slot = jnp.arange(NEST_DEV, dtype=jnp.int32)[None, None, :]
    first_block = (jnp.arange(block_count, dtype=jnp.int32) == 0)[None, :, None]
    step_off = 1 + (slot - bound + rotate) % (block_count - 1)
    owner = jnp.where(slot < bound, heavy, (heavy + step_off) % block_count)
    alive = (slot < bound) | (slot == bound) & first_block | (jax.random.randint(jax.random.fold_in(key, 23), shape, 0, 3) > 0)
    inside = jax.random.randint(jax.random.fold_in(key, 24), shape, 0, block_cells).astype(jnp.int32)
    in_last = (alive & (owner == block_count - 1)).astype(jnp.int32)
    first_last = (in_last > 0) & (jnp.cumsum(in_last, axis=2) == 1)
    inside = jnp.where(first_last, block_cells - 1, inside)
    values = jnp.where(alive, owner * block_cells + inside, -1).astype(jnp.int32)
    keys = jax.random.split(jax.random.fold_in(key, 25), row_count * block_count)
    orders = jax.vmap(lambda single: jax.random.permutation(single, NEST_DEV))(keys).reshape(shape)
    values = jnp.take_along_axis(values, orders.astype(jnp.int32), axis=2)
    return values.reshape(row_count, block_count * NEST_DEV).astype(jnp.int32)


def with_ends(array, key, low, largest):
    dims = array.shape
    index_at = [jax.random.randint(jax.random.fold_in(key, axis), (), 0, dims[axis]) for axis in range(len(dims))]
    array = array.at[tuple(index_at)].set(low)
    longest = dims.index(max(dims))
    index_at[longest] = (index_at[longest] + 1) % dims[longest]
    return array.at[tuple(index_at)].set(largest)


def block_levels(rng, shape, pieces, least, high):
    gain, own = 1.0, jax.random.fold_in(rng, 6)
    for dim, blocks in pieces:
        draws = jnp.exp(jax.random.uniform(jax.random.fold_in(own, dim), (blocks,), jnp.float32, least / len(pieces), high / len(pieces)))
        gain = gain * jnp.repeat(draws, shape[dim] // blocks).reshape([-1 if axis == dim else 1 for axis in range(len(shape))])
    return gain


def normal_values(own_key, dims, width, most, cuts=(), held_as=jnp.bfloat16):
    gain = block_levels(own_key, dims, cuts, -0.22, 0.18) if cuts else 1.0
    array = jax.random.normal(own_key, dims, jnp.float32) * width * gain
    return jnp.minimum(jnp.maximum(array, -most), most).astype(held_as)


def setup_inputs(seed: int = 0) -> dict:
    splits = jax.random.split(jax.random.key(seed), 8)
    tracer = normal_values(splits[0], (TRACER_TOTAL, DEPTH_LEVELS, NLAT, NLON), 1.0, 6.0, ((2, 4), (3, 8)), jnp.float32)
    velocity = normal_values(splits[1], (2, DEPTH_LEVELS, NLAT, NLON), 0.15, 2.0, ((2, 4), (3, 8)), jnp.float32)
    land_mask = with_ends((jax.random.randint(splits[2], (NLAT, NLON), 0, 4) < 3).astype(jnp.int32), jax.random.fold_in(splits[2], 1), 0, 1)
    fold_map = draw_fold_map(jax.random.fold_in(splits[7], 71), 0)
    nested_tracer_field = normal_values(splits[4], (TRACER_TOTAL, DEPTH_LEVELS, NEST_SLOT_ROWS, SLOTS_PER_ROW), 1.0, 6.0, ((2, 4), (3, 8)), jnp.float32)
    nested_cell_volume = jnp.clip(jnp.exp(math.log(0.2) - 1.3862944 * jax.random.uniform(splits[5], (NEST_SLOT_ROWS, SLOTS_PER_ROW), jnp.float32) ** block_levels(splits[5], (NEST_SLOT_ROWS, SLOTS_PER_ROW), ((0, 4), (1, 8)), -0.2, 0.2)), 0.05, 0.2)
    nest_parent = draw_nest_parent(jax.random.fold_in(splits[7], 71), 0)
    return {"tracer": tracer, "velocity": velocity, "land_mask": land_mask, "fold_map": fold_map, "nested_tracer_field": nested_tracer_field, "nested_cell_volume": nested_cell_volume, "nest_parent": nest_parent}


DIFFUSION = 0.15


def transport(ext_tracer, ext_east, ext_north, ext_ocean):
    middle_rows = ext_tracer[..., 1:-1, :]
    east_speed = 0.5 * (ext_east[:, 1:-1, :-1] + ext_east[:, 1:-1, 1:])
    east_open = ext_ocean[1:-1, :-1] * ext_ocean[1:-1, 1:]
    left_side = middle_rows[..., :-1]
    right_side = middle_rows[..., 1:]
    flux_east = east_open * (east_speed * 0.5 * (left_side + right_side) - DIFFUSION * (right_side - left_side))
    middle_cols = ext_tracer[..., :, 1:-1]
    north_speed = 0.5 * (ext_north[:, :-1, 1:-1] + ext_north[:, 1:, 1:-1])
    north_open = ext_ocean[:-1, 1:-1] * ext_ocean[1:, 1:-1]
    lower_side = middle_cols[..., :-1, :]
    upper_side = middle_cols[..., 1:, :]
    flux_north = north_open * (north_speed * 0.5 * (lower_side + upper_side) - DIFFUSION * (upper_side - lower_side))
    centre = ext_tracer[..., 1:-1, 1:-1]
    return centre - ((flux_east[..., 1:] - flux_east[..., :-1]) + (flux_north[..., 1:, :] - flux_north[..., :-1, :]))


def pad_field(field, top_row):
    extended = jnp.concatenate([jnp.zeros_like(field[..., :1, :]), field, top_row[..., None, :]], axis=-2)
    return jnp.concatenate([extended[..., -1:], extended, extended[..., :1]], axis=-1)


def reference(tracer, velocity, land_mask, fold_map, nested_tracer_field, nested_cell_volume, nest_parent):
    ocean_cells = land_mask.astype(jnp.float32)
    grid_rows, grid_cols = ocean_cells.shape
    ext_east = pad_field(velocity[0], -velocity[0][:, -1, :][:, fold_map])
    ext_north = pad_field(velocity[1], -velocity[1][:, -1, :][:, fold_map])
    ext_ocean = pad_field(ocean_cells, ocean_cells[-1, fold_map])
    block_cells = CLAT * CLON
    row_number = jnp.arange(NEST_SLOT_ROWS, dtype=jnp.int32)[:, None]
    inside = jnp.where(nest_parent >= 0, nest_parent, 0) % block_cells
    cell_row = row_number * CLAT + inside // CLON
    cell_col = (jnp.where(nest_parent >= 0, nest_parent, 0) // block_cells) * CLON + inside % CLON
    target = jnp.where(nest_parent >= 0, cell_row * grid_cols + cell_col, grid_rows * grid_cols).reshape(-1).astype(jnp.int32)
    volume_sum = jax.ops.segment_sum(nested_cell_volume.reshape(-1), target, num_segments=grid_rows * grid_cols)
    volume_sum = volume_sum.reshape(grid_rows, grid_cols)

    def one_tracer(tracer_index):
        field = tracer[tracer_index]
        ext_tracer = pad_field(field, field[:, -1, :][:, fold_map])
        advected = transport(ext_tracer, ext_east, ext_north, ext_ocean)
        masses = (nested_tracer_field[tracer_index] * nested_cell_volume).reshape(DEPTH_LEVELS, -1)
        mass_sum = jax.ops.segment_sum(masses.T, target, num_segments=grid_rows * grid_cols).T
        mass_sum = mass_sum.reshape(DEPTH_LEVELS, grid_rows, grid_cols)
        return (advected + mass_sum) / (1.0 + volume_sum)

    return lax.map(one_tracer, jnp.arange(TRACER_TOTAL, dtype=jnp.int32))
```

```python
import jax
import jax.numpy as jnp
from jax import lax
from jax.experimental import pallas as pl
from jax.experimental.pallas import tpu as pltpu
from jax.sharding import PartitionSpec as P

DIFFUSION = 0.15
LANES = 128
F32 = jnp.float32
BF16 = jnp.bfloat16
NT = (((1,), (1,)), ((), ()))


def halves(x):
    high = x.astype(BF16).astype(F32)
    return high, x - high


def iota(shape, dim):
    return lax.broadcasted_iota(jnp.int32, shape, dim)


def face(ocean_lo, ocean_hi, speed_lo, speed_hi, lo, hi):
    speed = 0.25 * (speed_lo + speed_hi)
    return ocean_lo * ocean_hi * (speed * (lo + hi) - DIFFUSION * (hi - lo))


def bucket_kernel(
    parent_ref, volume_ref, field_ref, out_ref, left_ref, hot_ref, *, count, bound, cells
):
    blocks = parent_ref.shape[0]
    channels = field_ref.shape[0] // blocks
    shift = cells.bit_length() - 1
    parent = parent_ref[...]
    owner = lax.shift_right_arithmetic(parent, shift)
    inside = (lax.bitwise_and(parent, cells - 1) + 1).astype(F32)
    member = jnp.concatenate([jnp.where(owner == d, 1.0, 0.0) for d in range(count)], axis=0)
    square = (LANES, LANES)
    before = jnp.where(iota(square, 0) < iota(square, 1), 1.0, 0.0).astype(BF16)
    within = jnp.dot(member.astype(BF16), before, preferred_element_type=F32)
    total = jnp.broadcast_to(jnp.sum(member, axis=1, keepdims=True), member.shape)
    rows = count * blocks
    one, two = iota((rows, rows), 0), iota((rows, rows), 1)
    bits = blocks.bit_length() - 1
    same = lax.shift_right_logical(one, bits) == lax.shift_right_logical(two, bits)
    earlier = jnp.where(same & (two < one), 1.0, 0.0).astype(BF16)
    place = within + jnp.dot(earlier, total.astype(BF16), preferred_element_type=F32)
    picked = place * member
    rank = picked[:blocks]
    for d in range(1, count):
        rank = rank + picked[d * blocks : (d + 1) * blocks]
    rank = jnp.where(parent >= 0, rank, -1.0).astype(jnp.int32)
    extra = count * 2 * channels
    for b in range(blocks):
        lanes = slice(b * LANES, (b + 1) * LANES)
        spots = iota((bound, LANES), 0)
        hot_ref[:, lanes] = jnp.where(spots == rank[b : b + 1], 1.0, 0.0).astype(BF16)
        volume = volume_ref[b : b + 1, :]
        mass = field_ref[pl.ds(b, channels, stride=blocks), :] * volume
        pair = jnp.concatenate(halves(mass), axis=0)
        mine = [member[d * blocks + b : d * blocks + b + 1] for d in range(count)]
        for d in range(count):
            left_ref[d * 2 * channels : (d + 1) * 2 * channels, lanes] = (pair * mine[d]).astype(BF16)
        mask = jnp.concatenate(mine, axis=0)
        small = [h * mask for x in (volume, inside[b : b + 1]) for h in halves(x)]
        left_ref[extra : extra + 4 * count, lanes] = jnp.concatenate(small, axis=0).astype(BF16)
    result = lax.dot_general(left_ref[...], hot_ref[...], NT, preferred_element_type=F32)
    pieces = bound // LANES
    volumes = result[extra : extra + count] + result[extra + count : extra + 2 * count]
    insides = (
        result[extra + 2 * count : extra + 3 * count] + result[extra + 3 * count : extra + 4 * count]
    )
    base = pieces * channels
    for d in range(count):
        top = d * 2 * channels
        mass = result[top : top + channels] + result[top + channels : top + 2 * channels]
        for k in range(pieces):
            lanes = slice(k * LANES, (k + 1) * LANES)
            out_ref[d, k * channels : (k + 1) * channels, :] = mass[:, lanes]
            out_ref[d, base + k : base + k + 1, :] = volumes[d : d + 1, lanes]
            out_ref[d, base + pieces + k : base + pieces + k + 1, :] = insides[d : d + 1, lanes]


def pack_kernel(tracer_ref, velocity_ref, mask_ref, west_ref, east_ref, a_ref, b_ref):
    channels, rows, columns = tracer_ref.shape
    levels = velocity_ref.shape[0] // 2
    ocean = mask_ref[...].astype(F32)
    lane = iota((rows, LANES), 1)
    for ref, at in ((west_ref, 0), (east_ref, columns - 1)):
        edge = slice(at, at + 1)
        packed = jnp.where(lane < 3 * channels, ocean[:, edge], 0.0)
        for n in range(levels):
            spot = (lane >= channels) & (lane < 2 * channels) & (lane % levels == n)
            packed = jnp.where(spot, velocity_ref[n, :, edge], packed)
        for n in range(channels):
            packed = jnp.where(lane == n, tracer_ref[n, :, edge], packed)
        ref[...] = packed
    odd = lax.axis_index("lat") % 2 == 1
    for top, n, ref in ((0, channels, tracer_ref), (channels, levels, velocity_ref)):
        start = 0 if top == 0 else levels
        first = ref[start : start + n, 0, :]
        last = ref[start : start + n, rows - 1, :]
        a_ref[top : top + n, :] = jnp.where(odd, last, first)
        b_ref[top : top + n, :] = jnp.where(odd, first, last)
    first = jnp.broadcast_to(ocean[0:1], (8, columns))
    last = jnp.broadcast_to(ocean[rows - 1 : rows], (8, columns))
    top = channels + levels
    a_ref[top : top + 8, :] = jnp.where(odd, last, first)
    b_ref[top : top + 8, :] = jnp.where(odd, first, last)


def stencil_kernel(
    tracer_ref, velocity_ref, mask_ref, fold_ref,
    west_ref, east_ref, a_ref, b_ref,
    from_west_ref, from_east_ref, from_a_ref, from_b_ref,
    out_ref,
):
    channels, rows, columns = tracer_ref.shape
    levels = velocity_ref.shape[0] // 2
    lat = lax.axis_index("lat")
    lon = lax.axis_index("lon")
    odd = lat % 2 == 1
    at_top = lat == lax.axis_size("lat") - 1
    def columns_of(m):
        return (
            pltpu.roll(m, LANES - 2 * channels, 1),
            pltpu.roll(m, LANES - channels, 1),
            m,
        )

    def column_face(lo, hi):
        ocean_lo, speed_lo, c_lo = columns_of(lo)
        ocean_hi, speed_hi, c_hi = columns_of(hi)
        return face(ocean_lo, ocean_hi, speed_lo, speed_hi, c_lo, c_hi)

    flux_west = column_face(from_west_ref[...], west_ref[...])
    flux_east = column_face(east_ref[...], from_east_ref[...])
    first = jnp.where(odd, b_ref[...], a_ref[...])
    last = jnp.where(odd, a_ref[...], b_ref[...])
    north = jnp.where(odd, from_a_ref[...], from_b_ref[...])
    south = jnp.where(odd, from_b_ref[...], from_a_ref[...])
    count = lax.axis_size("lon")
    partner = fold_ref[...] - (count - 1 - lon) * columns
    pick = jnp.where(iota((columns, columns), 0) == partner, 1.0, 0.0).astype(BF16)
    high, rest = halves(north)
    middle, low = halves(rest)
    folded = sum(
        jnp.dot(x.astype(BF16), pick, preferred_element_type=F32) for x in (high, middle, low)
    )
    turn = jnp.where(iota(folded.shape, 0) // levels == channels // levels, -1.0, 1.0)
    north = jnp.where(at_top, folded * turn, north)

    def row_parts(m):
        speed = jnp.concatenate([m[channels : channels + levels]] * (channels // levels), axis=0)
        ocean = jnp.broadcast_to(m[channels + levels : channels + levels + 1], (channels, columns))
        return ocean, speed, m[:channels]

    def row_face(lo, hi):
        ocean_lo, speed_lo, c_lo = row_parts(lo)
        ocean_hi, speed_hi, c_hi = row_parts(hi)
        return face(ocean_lo, ocean_hi, speed_lo, speed_hi, c_lo, c_hi)

    flux_north = row_face(last, north)
    flux_south = row_face(south, first)
    ocean = mask_ref[...].astype(F32)
    lane = iota((rows, columns), 1)
    row = iota((rows, columns), 0)
    open_east = jnp.where(lane == columns - 1, 0.0, ocean * pltpu.roll(ocean, columns - 1, 1))
    open_north = jnp.where(row == rows - 1, 0.0, ocean * pltpu.roll(ocean, rows - 1, 0))
    for level in range(levels):
        u = velocity_ref[level]
        v = velocity_ref[levels + level]
        u = 0.25 * (u + pltpu.roll(u, columns - 1, 1))
        v = 0.25 * (v + pltpu.roll(v, rows - 1, 0))
        for n in range(level, channels, levels):
            c = tracer_ref[n]
            c_e = pltpu.roll(c, columns - 1, 1)
            c_n = pltpu.roll(c, rows - 1, 0)
            f_e = open_east * (u * (c + c_e) - DIFFUSION * (c_e - c))
            f_n = open_north * (v * (c + c_n) - DIFFUSION * (c_n - c))
            f_w = jnp.where(lane == 0, flux_west[:, n : n + 1], pltpu.roll(f_e, 1, 1))
            f_e = jnp.where(lane == columns - 1, flux_east[:, n : n + 1], f_e)
            f_s = jnp.where(row == 0, flux_south[n : n + 1], pltpu.roll(f_n, 1, 0))
            f_n = jnp.where(row == rows - 1, flux_north[n : n + 1], f_n)
            out_ref[n] = c - ((f_e - f_w) + (f_n - f_s))


def scatter_kernel(slot_ref, advected_ref, out_ref, left_ref, hot_ref, *, bound):
    channels, rows, columns = advected_ref.shape
    count = slot_ref.shape[0]
    pieces = bound // LANES
    base = pieces * channels
    bits = columns.bit_length() - 1
    slots = count * bound
    for j in range(count):
        for k in range(pieces):
            at = (j * pieces + k) * LANES
            here = slice(at, at + LANES)
            there = slice(slots + at, slots + at + LANES)
            spot = slot_ref[j, base + pieces + k : base + pieces + k + 1, :]
            spot = spot.astype(jnp.int32) - 1
            spot_row = lax.shift_right_arithmetic(spot, bits)
            spot_column = lax.bitwise_and(spot, columns - 1)
            hot = jnp.where(iota((columns, LANES), 0) == spot_column, 1.0, 0.0).astype(BF16)
            hot_ref[:, here] = hot
            hot_ref[:, there] = hot
            in_row = jnp.where(iota((rows, LANES), 0) == spot_row, 1.0, 0.0).astype(BF16)
            mass = slot_ref[j, k * channels : (k + 1) * channels, :]
            volume = slot_ref[j, base + k : base + k + 1, :]
            for x, top, n in ((mass, 0, channels), (volume, channels, 1)):
                for part, to in zip(halves(x), (here, there)):
                    for i in range(n):
                        spread = jnp.broadcast_to(part[i : i + 1], (16, LANES)).astype(BF16)
                        spread = jnp.concatenate([spread] * (rows // 16), axis=0)
                        left_ref[(top + i) * rows : (top + i + 1) * rows, to] = spread * in_row
    volume = lax.dot_general(
        left_ref[channels * rows :, :], hot_ref[...], NT, preferred_element_type=F32
    )
    scale = 1.0 / (1.0 + volume)
    group = 8
    for n in range(0, channels, group):
        mass = lax.dot_general(
            left_ref[n * rows : (n + group) * rows, :], hot_ref[...], NT, preferred_element_type=F32
        )
        for i in range(group):
            out_ref[n + i] = (advected_ref[n + i] + mass[i * rows : (i + 1) * rows]) * scale


VMEM = pl.BlockSpec(memory_space=pltpu.VMEM)


def call(kernel, name, outs, *args, scratch=()):
    single = not isinstance(outs, (list, tuple))
    return pl.pallas_call(
        kernel,
        out_shape=outs,
        in_specs=[VMEM] * len(args),
        out_specs=VMEM if single else [VMEM] * len(outs),
        scratch_shapes=list(scratch),
        compiler_params=pltpu.CompilerParams(vmem_limit_bytes=48 << 20),
        name=name,
    )(*args)


def routes(lat_count, lon_count):
    first, second = [], []
    for lon in range(lon_count):
        for lat in range(lat_count):
            here = lon * lat_count + lat
            second.append((here, lon * lat_count + (lat ^ 1)))
            if lat == lat_count - 1:
                first.append((here, (lon_count - 1 - lon) * lat_count + lat))
            elif lat > 0:
                first.append((here, lon * lat_count + ((lat + 1) ^ 1) - 1))
    return first, second


def body(
    tracer, velocity, land_mask, fold_map, nested_tracer_field, nested_cell_volume, nest_parent
):
    tracers, levels, rows, columns = tracer.shape
    channels = tracers * levels
    lon_count, lat_count = lax.axis_size("lon"), lax.axis_size("lat")
    slot_count = nest_parent.shape[1]
    bound = 2 * slot_count // lon_count
    blocks = slot_count // LANES
    pieces = bound // LANES
    f32 = lambda *shape: jax.ShapeDtypeStruct(shape, F32)
    buckets = call(
        lambda *refs: bucket_kernel(*refs, count=lon_count, bound=bound, cells=rows * columns),
        "bucket",
        f32(lon_count, pieces * (channels + 2), LANES),
        nest_parent.reshape(blocks, LANES),
        nested_cell_volume.reshape(blocks, LANES),
        nested_tracer_field.reshape(channels * blocks, LANES),
        scratch=[
            pltpu.VMEM((lon_count * (2 * channels + 4), slot_count), BF16),
            pltpu.VMEM((bound, slot_count), BF16),
        ],
    )
    arrived = lax.all_to_all(buckets, "lon", 0, 0)
    c = tracer.reshape(channels, rows, columns)
    speed = velocity.reshape(2 * levels, rows, columns)
    edge, line = f32(rows, LANES), f32(channels + levels + 8, columns)
    west, east, to_a, to_b = call(
        pack_kernel, "pack", [edge, edge, line, line], c, speed, land_mask
    )
    up = [(i, (i + 1) % lon_count) for i in range(lon_count)]
    down = [(j, i) for i, j in up]
    first, second = routes(lat_count, lon_count)
    from_west = lax.ppermute(east, "lon", up)
    from_east = lax.ppermute(west, "lon", down)
    from_a = lax.ppermute(to_a, ("lon", "lat"), first)
    from_b = lax.ppermute(to_b, ("lon", "lat"), second)
    grid = f32(channels, rows, columns)
    advected = call(
        stencil_kernel, "stencil", grid, c, speed, land_mask, fold_map.reshape(1, columns),
        west, east, to_a, to_b, from_west, from_east, from_a, from_b,
    )
    after = call(
        lambda *refs: scatter_kernel(*refs, bound=bound),
        "scatter",
        grid,
        arrived,
        advected,
        scratch=[
            pltpu.VMEM(((channels + 1) * rows, 2 * lon_count * bound), BF16),
            pltpu.VMEM((columns, 2 * lon_count * bound), BF16),
        ],
    )
    return after.reshape(tracer.shape)


def solution(mesh):
    in_specs = (
        P(None, None, "lat", "lon"),
        P(None, None, "lat", "lon"),
        P("lat", "lon"),
        P("lon"),
        P(None, None, "lat", "lon"),
        P("lat", "lon"),
        P("lat", "lon"),
    )
    out_specs = P(None, None, "lat", "lon")
    return jax.shard_map(body, mesh=mesh, in_specs=in_specs, out_specs=out_specs, check_vma=False)
```

```python
import jax
import jax.numpy as jnp
from jax import lax
from jax.experimental import pallas as pl
from jax.experimental.pallas import tpu as pltpu
from jax.sharding import PartitionSpec as P

DIFFUSION = 0.15
LANES = 128
LIMIT = 32 << 20
SCALE = 1e9
DEPTH = 5
F32 = jnp.float32
BF16 = jnp.bfloat16
NT = (((1,), (1,)), ((), ()))


def halves(x):
    high = x.astype(BF16).astype(F32)
    return high, x - high


def iota(shape, dim):
    return lax.broadcasted_iota(jnp.int32, shape, dim)


def face(ocean_lo, ocean_hi, speed_lo, speed_hi, lo, hi):
    speed = 0.25 * (speed_lo + speed_hi)
    return ocean_lo * ocean_hi * (speed * (lo + hi) - DIFFUSION * (hi - lo))


def prepare_kernel(*refs, count, bound, cells, carriers):
    sources, out_refs, edge_refs = refs[:6], refs[6 : 6 + count], refs[6 + count : 10 + count]
    held, (left_ref, hot_ref, sems) = refs[10 + count : 16 + count], refs[16 + count :]
    copies = [
        pltpu.make_async_copy(source, ref, sems.at[n])
        for n, (source, ref) in enumerate(zip(sources, held))
    ]
    for copy in copies:
        copy.start()
    copies[0].wait()
    parent_ref, volume_ref, field_ref, *grid_refs = held
    blocks = parent_ref.shape[0]
    channels = field_ref.shape[0] // blocks
    shift = cells.bit_length() - 1
    parent = parent_ref[...]
    me = lax.axis_index("lon")
    owner = lax.bitwise_xor(lax.shift_right_arithmetic(parent, shift), me)
    owner = jnp.where(parent >= 0, owner, -1)
    inside = (lax.bitwise_and(parent, cells - 1) + 1).astype(F32)
    member = jnp.concatenate([jnp.where(owner == d, 1.0, 0.0) for d in range(count)], axis=0)
    square = (LANES, LANES)
    before = jnp.where(iota(square, 0) < iota(square, 1), 1.0, 0.0).astype(BF16)
    within = jnp.dot(member.astype(BF16), before, preferred_element_type=F32)
    total = jnp.broadcast_to(jnp.sum(member, axis=1, keepdims=True), member.shape)
    rows = count * blocks
    one, two = iota((rows, rows), 0), iota((rows, rows), 1)
    bits = blocks.bit_length() - 1
    same = lax.shift_right_logical(one, bits) == lax.shift_right_logical(two, bits)
    earlier = jnp.where(same & (two < one), 1.0, 0.0).astype(BF16)
    place = within + jnp.dot(earlier, total.astype(BF16), preferred_element_type=F32)
    picked = place * member
    rank = picked[:blocks]
    for d in range(1, count):
        rank = rank + picked[d * blocks : (d + 1) * blocks]
    rank = jnp.where(parent >= 0, rank, -1.0).astype(jnp.int32)
    extra = count * 2 * channels
    copies[1].wait()
    copies[2].wait()
    for b in range(blocks):
        lanes = slice(b * LANES, (b + 1) * LANES)
        spots = iota((bound, LANES), 0)
        hot_ref[:, lanes] = jnp.where(spots == rank[b : b + 1], 1.0, 0.0).astype(BF16)
        volume = volume_ref[b : b + 1, :]
        mass = field_ref[pl.ds(b, channels, stride=blocks), :] * volume
        pair = jnp.concatenate(halves(mass), axis=0)
        mine = [member[d * blocks + b : d * blocks + b + 1] for d in range(count)]
        for d in range(count):
            left_ref[d * 2 * channels : (d + 1) * 2 * channels, lanes] = (pair * mine[d]).astype(BF16)
        mask = jnp.concatenate(mine, axis=0)
        small = [h * mask for x in (volume, inside[b : b + 1]) for h in halves(x)]
        left_ref[extra : extra + 4 * count, lanes] = jnp.concatenate(small, axis=0).astype(BF16)
    result = lax.dot_general(left_ref[...], hot_ref[...], NT, preferred_element_type=F32)
    pieces = bound // LANES
    volumes = result[extra : extra + count] + result[extra + count : extra + 2 * count]
    insides = (
        result[extra + 2 * count : extra + 3 * count] + result[extra + 3 * count : extra + 4 * count]
    )
    base = pieces * channels
    for d in range(count):
        top = d * 2 * channels
        mass = result[top : top + channels] + result[top + channels : top + 2 * channels]
        for k in range(pieces):
            lanes = slice(k * LANES, (k + 1) * LANES)
            out_refs[d][k * channels : (k + 1) * channels, :] = mass[:, lanes]
            out_refs[d][base + k : base + k + 1, :] = volumes[d : d + 1, lanes]
            out_refs[d][base + pieces + k : base + pieces + k + 1, :] = insides[d : d + 1, lanes]
    for copy in copies[3:]:
        copy.wait()
    pack_edges(*grid_refs, {k: out_refs[k] for k in carriers}, *edge_refs, count)


def pack_edges(tracer_ref, velocity_ref, mask_ref, message_refs, west_ref, east_ref, a_ref, b_ref, count):
    channels, rows, columns = tracer_ref.shape
    levels = velocity_ref.shape[0] // 2
    ocean = mask_ref[...].astype(F32)
    lane = iota((rows, LANES), 1)
    for ref, at in ((west_ref, 0), (east_ref, columns - 1)):
        edge = slice(at, at + 1)
        packed = jnp.where(lane < 3 * channels, ocean[:, edge], 0.0)
        for n in range(levels):
            spot = (lane >= channels) & (lane < 2 * channels) & (lane % levels == n)
            packed = jnp.where(spot, velocity_ref[n, :, edge], packed)
        for n in range(channels):
            packed = jnp.where(lane == n, tracer_ref[n, :, edge], packed)
        ref[...] = packed
    me = lax.axis_index("lon")
    for k, ref in message_refs.items():
        is_west = lax.bitwise_xor(me, k) == (me + count - 1) % count
        ref[ref.shape[0] - rows :, :] = jnp.where(is_west, west_ref[...], east_ref[...])
    odd = lax.axis_index("lat") % 2 == 1
    for top, n, ref in ((0, channels, tracer_ref), (channels, levels, velocity_ref)):
        start = 0 if top == 0 else levels
        first = ref[start : start + n, 0, :]
        last = ref[start : start + n, rows - 1, :]
        a_ref[top : top + n, :] = jnp.where(odd, last, first)
        b_ref[top : top + n, :] = jnp.where(odd, first, last)
    first = jnp.broadcast_to(ocean[0:1], (8, columns))
    last = jnp.broadcast_to(ocean[rows - 1 : rows], (8, columns))
    top = channels + levels
    a_ref[top : top + 8, :] = jnp.where(odd, last, first)
    b_ref[top : top + 8, :] = jnp.where(odd, first, last)


def stencil_kernel(
    tracer_ref, velocity_ref, mask_ref, fold_ref,
    west_ref, east_ref, a_ref, b_ref, from_a_ref, from_b_ref, *refs, carriers,
):
    message_refs, out_ref = refs[:-1], refs[-1]
    channels, rows, columns = tracer_ref.shape
    levels = velocity_ref.shape[0] // 2
    lat = lax.axis_index("lat")
    lon = lax.axis_index("lon")
    odd = lat % 2 == 1
    at_top = lat == lax.axis_size("lat") - 1
    def columns_of(m):
        return (
            pltpu.roll(m, LANES - 2 * channels, 1),
            pltpu.roll(m, LANES - channels, 1),
            m,
        )

    def column_face(lo, hi):
        ocean_lo, speed_lo, c_lo = columns_of(lo)
        ocean_hi, speed_hi, c_hi = columns_of(hi)
        return face(ocean_lo, ocean_hi, speed_lo, speed_hi, c_lo, c_hi)

    count = lax.axis_size("lon")
    edges = [ref[ref.shape[0] - rows :, :] for ref in message_refs]
    from_west, from_east = edges[0], edges[0]
    for k, edge in zip(carriers[1:], edges[1:]):
        partner = lax.bitwise_xor(lon, k)
        from_west = jnp.where(partner == (lon + count - 1) % count, edge, from_west)
        from_east = jnp.where(partner == (lon + 1) % count, edge, from_east)
    flux_west = column_face(from_west, west_ref[...])
    flux_east = column_face(east_ref[...], from_east)
    first = jnp.where(odd, b_ref[...], a_ref[...])
    last = jnp.where(odd, a_ref[...], b_ref[...])
    north = jnp.where(odd, from_a_ref[...], from_b_ref[...])
    south = jnp.where(odd, from_b_ref[...], from_a_ref[...])
    partner = fold_ref[...] - (count - 1 - lon) * columns
    pick = jnp.where(iota((columns, columns), 0) == partner, 1.0, 0.0).astype(BF16)
    high, rest = halves(north)
    middle, low = halves(rest)
    folded = sum(
        jnp.dot(x.astype(BF16), pick, preferred_element_type=F32) for x in (high, middle, low)
    )
    turn = jnp.where(iota(folded.shape, 0) // levels == channels // levels, -1.0, 1.0)
    north = jnp.where(at_top, folded * turn, north)

    def row_parts(m):
        speed = jnp.concatenate([m[channels : channels + levels]] * (channels // levels), axis=0)
        ocean = jnp.broadcast_to(m[channels + levels : channels + levels + 1], (channels, columns))
        return ocean, speed, m[:channels]

    def row_face(lo, hi):
        ocean_lo, speed_lo, c_lo = row_parts(lo)
        ocean_hi, speed_hi, c_hi = row_parts(hi)
        return face(ocean_lo, ocean_hi, speed_lo, speed_hi, c_lo, c_hi)

    flux_north = row_face(last, north)
    flux_south = row_face(south, first)
    ocean = mask_ref[...].astype(F32)
    lane = iota((rows, columns), 1)
    row = iota((rows, columns), 0)
    open_east = jnp.where(lane == columns - 1, 0.0, ocean * pltpu.roll(ocean, columns - 1, 1))
    open_north = jnp.where(row == rows - 1, 0.0, ocean * pltpu.roll(ocean, rows - 1, 0))
    for level in range(levels):
        u = velocity_ref[level]
        v = velocity_ref[levels + level]
        u = 0.25 * (u + pltpu.roll(u, columns - 1, 1))
        v = 0.25 * (v + pltpu.roll(v, rows - 1, 0))
        for n in range(level, channels, levels):
            c = tracer_ref[n]
            c_e = pltpu.roll(c, columns - 1, 1)
            c_n = pltpu.roll(c, rows - 1, 0)
            f_e = open_east * (u * (c + c_e) - DIFFUSION * (c_e - c))
            f_n = open_north * (v * (c + c_n) - DIFFUSION * (c_n - c))
            f_w = jnp.where(lane == 0, flux_west[:, n : n + 1], pltpu.roll(f_e, 1, 1))
            f_e = jnp.where(lane == columns - 1, flux_east[:, n : n + 1], f_e)
            f_s = jnp.where(row == 0, flux_south[n : n + 1], pltpu.roll(f_n, 1, 0))
            f_n = jnp.where(row == rows - 1, flux_north[n : n + 1], f_n)
            out_ref[n] = c - ((f_e - f_w) + (f_n - f_s))


def scatter_kernel(*refs, messages, first, last, join, bound, shape):
    channels, rows, columns = shape
    slot_refs, refs = refs[:messages], refs[messages:]
    sum_ref, refs = (None, refs) if first else (refs[0], refs[1:])
    advected_ref, refs = (refs[0], refs[1:]) if join else (None, refs)
    out_ref, left_ref, hot_ref = refs
    pieces = bound // LANES
    base = pieces * channels
    bits = columns.bit_length() - 1
    slots = messages * bound
    for j, slot_ref in enumerate(slot_refs):
        for k in range(pieces):
            at = (j * pieces + k) * LANES
            here = slice(at, at + LANES)
            there = slice(slots + at, slots + at + LANES)
            spot = slot_ref[base + pieces + k : base + pieces + k + 1, :].astype(jnp.int32) - 1
            spot_row = lax.shift_right_arithmetic(spot, bits)
            spot_column = lax.bitwise_and(spot, columns - 1)
            hot = jnp.where(iota((columns, LANES), 0) == spot_column, 1.0, 0.0).astype(BF16)
            hot_ref[:, here] = hot
            hot_ref[:, there] = hot
            in_row = jnp.where(iota((rows, LANES), 0) == spot_row, 1.0, 0.0).astype(BF16)
            mass = slot_ref[k * channels : (k + 1) * channels, :]
            volume = slot_ref[base + k : base + k + 1, :]
            for x, top, n in ((mass, 0, channels), (volume, channels, 1)):
                for part, to in zip(halves(x), (here, there)):
                    for i in range(n):
                        spread = jnp.broadcast_to(part[i : i + 1], (16, LANES)).astype(BF16)
                        spread = jnp.concatenate([spread] * (rows // 16), axis=0)
                        left_ref[(top + i) * rows : (top + i + 1) * rows, to] = spread * in_row

    def summed(n, size):
        part = slice(n * rows, (n + size) * rows)
        new = lax.dot_general(left_ref[part, :], hot_ref[...], NT, preferred_element_type=F32)
        new = new if first else sum_ref[part, :] + new
        if join and n < channels:
            new = new + advected_ref[n : n + size].reshape(size * rows, columns)
        return new

    volume = summed(channels, 1)
    if last:
        scale = 1.0 / (1.0 + volume)
    else:
        out_ref[channels * rows :, :] = volume
    group = 8
    for n in range(0, channels, group):
        mass = summed(n, group)
        if last:
            for i in range(group):
                out_ref[n + i] = mass[i * rows : (i + 1) * rows] * scale
        else:
            out_ref[n * rows : (n + group) * rows, :] = mass


VMEM = pl.BlockSpec(memory_space=pltpu.VMEM)


HBM = pl.BlockSpec(memory_space=pltpu.MemorySpace.HBM)


def cost(microseconds):
    return pl.CostEstimate(flops=int(SCALE * microseconds), bytes_accessed=0, transcendentals=0)


def call(kernel, name, outs, *args, scratch=(), specs=None, aliases=None, cost=None):
    single = not isinstance(outs, (list, tuple))
    return pl.pallas_call(
        kernel,
        out_shape=outs,
        in_specs=specs or [VMEM] * len(args),
        out_specs=VMEM if single else [VMEM] * len(outs),
        scratch_shapes=list(scratch),
        input_output_aliases=aliases or {},
        compiler_params=pltpu.CompilerParams(vmem_limit_bytes=LIMIT),
        cost_estimate=cost,
        name=name,
    )(*args)


def SEQUENCE(count):
    far = list(range(count // 2, count - 1))
    near = [k for k in range(1, count // 2) if k & (k + 1)]
    carriers = [k for k in range(1, count // 2) if not k & (k + 1)]
    return ["b", "a", count - 1, far[0], *carriers, *far[1:], *near]


def GROUPS(sequence):
    groups = [[0]] + [[k] for k in sequence if k not in ("a", "b")]
    return groups, len(groups) - 3


def routes(lat_count, lon_count):
    first, second = [], []
    for lon in range(lon_count):
        for lat in range(lat_count):
            here = lon * lat_count + lat
            second.append((here, lon * lat_count + (lat ^ 1)))
            if lat == lat_count - 1:
                first.append((here, (lon_count - 1 - lon) * lat_count + lat))
            elif lat > 0:
                first.append((here, lon * lat_count + ((lat + 1) ^ 1) - 1))
    return first, second


def body(
    tracer, velocity, land_mask, fold_map, nested_tracer_field, nested_cell_volume, nest_parent
):
    tracers, levels, rows, columns = tracer.shape
    channels = tracers * levels
    lon_count, lat_count = lax.axis_size("lon"), lax.axis_size("lat")
    slot_count = nest_parent.shape[1]
    bound = 2 * slot_count // lon_count
    blocks = slot_count // LANES
    pieces = bound // LANES
    f32 = lambda *shape: jax.ShapeDtypeStruct(shape, F32)
    size = pieces * (channels + 2)
    carriers = [k for k in range(1, lon_count) if k & (k + 1) == 0]
    heights = [size + rows if k in carriers else size for k in range(lon_count)]
    c = tracer.reshape(channels, rows, columns)
    speed = velocity.reshape(2 * levels, rows, columns)
    edge, line = f32(rows, LANES), f32(channels + levels + 8, columns)
    inputs = (
        nest_parent.reshape(blocks, LANES),
        nested_cell_volume.reshape(blocks, LANES),
        nested_tracer_field.reshape(channels * blocks, LANES),
        c, speed, land_mask,
    )
    results = call(
        lambda *refs: prepare_kernel(
            *refs, count=lon_count, bound=bound, cells=rows * columns, carriers=carriers
        ),
        "prepare",
        [f32(height, LANES) for height in heights] + [edge, edge, line, line],
        *[pltpu.with_memory_space_constraint(x, pltpu.MemorySpace.HBM) for x in inputs],
        specs=[HBM] * len(inputs),
        scratch=[pltpu.VMEM(x.shape, x.dtype) for x in inputs]
        + [
            pltpu.VMEM((lon_count * (2 * channels + 4), slot_count), BF16),
            pltpu.VMEM((bound, slot_count), BF16),
            pltpu.SemaphoreType.DMA((len(inputs),)),
        ],
    )
    buckets, (west, east, to_a, to_b) = results[:lon_count], results[lon_count:]
    arrived = {0: buckets[0]}
    first, second = routes(lat_count, lon_count)
    pair = lambda k: [(i, i ^ k) for i in range(lon_count)]
    sends = {k: (buckets[k], "lon", pair(k)) for k in range(1, lon_count)}
    sends["a"] = (to_a, ("lon", "lat"), first)
    sends["b"] = (to_b, ("lon", "lat"), second)
    sequence = SEQUENCE(lon_count)
    for n, key in enumerate(sequence):
        block, axes, pairs = sends[key]
        if n >= DEPTH:
            ahead = sequence[n - DEPTH]
            block, arrived[ahead] = lax.optimization_barrier((block, arrived[ahead]))
        arrived[key] = lax.ppermute(block, axes, pairs)
    grid = f32(channels, rows, columns)
    advected = call(
        lambda *refs: stencil_kernel(*refs, carriers=carriers),
        "stencil", grid, c, speed, land_mask, fold_map.reshape(1, columns),
        west, east, to_a, to_b, arrived["a"], arrived["b"], *[arrived[k] for k in carriers],
        cost=cost(3),
    )
    groups, joins = GROUPS(sequence)
    total = None
    for n, group in enumerate(groups):
        last = n == len(groups) - 1
        start = total is None
        join = n == joins
        args = [arrived[k] for k in group] + ([] if start else [total]) + ([advected] if join else [])
        total = call(
            lambda *refs: scatter_kernel(
                *refs, messages=len(group), first=start, last=last, join=join, bound=bound,
                shape=(channels, rows, columns),
            ),
            "scatter",
            grid if last else f32((channels + 1) * rows, columns),
            *args,
            aliases={} if start or last else {len(group): 0},
            scratch=[
                pltpu.VMEM(((channels + 1) * rows, 2 * len(group) * bound), BF16),
                pltpu.VMEM((columns, 2 * len(group) * bound), BF16),
            ],
            cost=cost(len(group)),
        )
    return total.reshape(tracer.shape)


def solution(mesh):
    in_specs = (
        P(None, None, "lat", "lon"),
        P(None, None, "lat", "lon"),
        P("lat", "lon"),
        P("lon"),
        P(None, None, "lat", "lon"),
        P("lat", "lon"),
        P("lat", "lon"),
    )
    out_specs = P(None, None, "lat", "lon")
    return jax.shard_map(body, mesh=mesh, in_specs=in_specs, out_specs=out_specs, check_vma=False)
```

```python
import jax
import jax.numpy as jnp
from jax import lax
from jax.experimental import pallas as pl
from jax.experimental.pallas import tpu as pltpu
from jax.sharding import PartitionSpec as P

DIFFUSION = 0.15
LANES = 128
LIMIT = 32 << 20
SCALE = 1e9
DEPTH = 5
F32 = jnp.float32
BF16 = jnp.bfloat16
NT = (((1,), (1,)), ((), ()))


def halves(x):
    high = x.astype(BF16).astype(F32)
    return high, x - high


def iota(shape, dim):
    return lax.broadcasted_iota(jnp.int32, shape, dim)


def prepare_kernel(*refs, count, bound, cells, carriers):
    sources, out_refs, edge_refs = refs[:6], refs[6 : 6 + count], refs[6 + count : 8 + count]
    held, (left_ref, hot_ref, sems) = refs[8 + count : 14 + count], refs[14 + count :]
    copies = [
        pltpu.make_async_copy(source, ref, sems.at[n])
        for n, (source, ref) in enumerate(zip(sources, held))
    ]
    for copy in copies:
        copy.start()
    copies[0].wait()
    parent_ref, volume_ref, field_ref, *grid_refs = held
    blocks = parent_ref.shape[0]
    channels = field_ref.shape[0] // blocks
    shift = cells.bit_length() - 1
    parent = parent_ref[...]
    me = lax.axis_index("lon")
    owner = lax.bitwise_xor(lax.shift_right_arithmetic(parent, shift), me)
    owner = jnp.where(parent >= 0, owner, -1)
    inside = (lax.bitwise_and(parent, cells - 1) + 1).astype(F32)
    member = jnp.concatenate([jnp.where(owner == d, 1.0, 0.0) for d in range(count)], axis=0)
    square = (LANES, LANES)
    before = jnp.where(iota(square, 0) < iota(square, 1), 1.0, 0.0).astype(BF16)
    within = jnp.dot(member.astype(BF16), before, preferred_element_type=F32)
    total = jnp.broadcast_to(jnp.sum(member, axis=1, keepdims=True), member.shape)
    rows = count * blocks
    one, two = iota((rows, rows), 0), iota((rows, rows), 1)
    bits = blocks.bit_length() - 1
    same = lax.shift_right_logical(one, bits) == lax.shift_right_logical(two, bits)
    earlier = jnp.where(same & (two < one), 1.0, 0.0).astype(BF16)
    place = within + jnp.dot(earlier, total.astype(BF16), preferred_element_type=F32)
    picked = place * member
    rank = picked[:blocks]
    for d in range(1, count):
        rank = rank + picked[d * blocks : (d + 1) * blocks]
    rank = jnp.where(parent >= 0, rank, -1.0).astype(jnp.int32)
    extra = count * 2 * channels
    copies[1].wait()
    copies[2].wait()
    for b in range(blocks):
        lanes = slice(b * LANES, (b + 1) * LANES)
        spots = iota((bound, LANES), 0)
        hot_ref[:, lanes] = jnp.where(spots == rank[b : b + 1], 1.0, 0.0).astype(BF16)
        volume = volume_ref[b : b + 1, :]
        mass = field_ref[pl.ds(b, channels, stride=blocks), :] * volume
        pair = jnp.concatenate(halves(mass), axis=0)
        mine = [member[d * blocks + b : d * blocks + b + 1] for d in range(count)]
        for d in range(count):
            left_ref[d * 2 * channels : (d + 1) * 2 * channels, lanes] = (pair * mine[d]).astype(BF16)
        mask = jnp.concatenate(mine, axis=0)
        small = [h * mask for x in (volume, inside[b : b + 1]) for h in halves(x)]
        left_ref[extra : extra + 4 * count, lanes] = jnp.concatenate(small, axis=0).astype(BF16)
    result = lax.dot_general(left_ref[...], hot_ref[...], NT, preferred_element_type=F32)
    pieces = bound // LANES
    volumes = result[extra : extra + count] + result[extra + count : extra + 2 * count]
    insides = (
        result[extra + 2 * count : extra + 3 * count] + result[extra + 3 * count : extra + 4 * count]
    )
    base = pieces * channels
    for d in range(count):
        top = d * 2 * channels
        mass = result[top : top + channels] + result[top + channels : top + 2 * channels]
        for k in range(pieces):
            lanes = slice(k * LANES, (k + 1) * LANES)
            out_refs[d][k * channels : (k + 1) * channels, :] = mass[:, lanes]
            out_refs[d][base + k : base + k + 1, :] = volumes[d : d + 1, lanes]
            out_refs[d][base + pieces + k : base + pieces + k + 1, :] = insides[d : d + 1, lanes]
    for copy in copies[3:]:
        copy.wait()
    pack_edges(*grid_refs, {k: out_refs[k] for k in carriers}, *edge_refs, count)


def pack_edges(tracer_ref, velocity_ref, mask_ref, message_refs, a_ref, b_ref, count):
    channels, rows, columns = tracer_ref.shape
    levels = velocity_ref.shape[0] // 2
    ocean = mask_ref[...].astype(F32)
    lane = iota((rows, LANES), 1)
    edges = []
    for at in (0, columns - 1):
        edge = slice(at, at + 1)
        packed = jnp.where(lane < 3 * channels, ocean[:, edge], 0.0)
        for n in range(levels):
            spot = (lane >= channels) & (lane < 2 * channels) & (lane % levels == n)
            packed = jnp.where(spot, velocity_ref[n, :, edge], packed)
        for n in range(channels):
            packed = jnp.where(lane == n, tracer_ref[n, :, edge], packed)
        edges.append(packed)
    me = lax.axis_index("lon")
    for k, ref in message_refs.items():
        is_west = lax.bitwise_xor(me, k) == (me + count - 1) % count
        ref[ref.shape[0] - rows :, :] = jnp.where(is_west, edges[0], edges[1])
    odd = lax.axis_index("lat") % 2 == 1
    for top, n, ref in ((0, channels, tracer_ref), (channels, levels, velocity_ref)):
        start = 0 if top == 0 else levels
        first = ref[start : start + n, 0, :]
        last = ref[start : start + n, rows - 1, :]
        a_ref[top : top + n, :] = jnp.where(odd, last, first)
        b_ref[top : top + n, :] = jnp.where(odd, first, last)
    first = jnp.broadcast_to(ocean[0:1], (8, columns))
    last = jnp.broadcast_to(ocean[rows - 1 : rows], (8, columns))
    top = channels + levels
    a_ref[top : top + 8, :] = jnp.where(odd, last, first)
    b_ref[top : top + 8, :] = jnp.where(odd, first, last)


def shifted(x, west, east, south, north):
    rows, columns = x.shape
    lane = iota((rows, LANES), 1)
    row = iota((rows, columns), 0)
    tiles = [x[:, at : at + LANES] for at in range(0, columns, LANES)]
    left = [pltpu.roll(t, LANES - 1, 1) for t in tiles] + [east]
    right = [west] + [pltpu.roll(t, 1, 1) for t in tiles]
    pairs = range(len(tiles))
    return (
        jnp.concatenate([jnp.where(lane > 0, right[i + 1], right[i]) for i in pairs], axis=1),
        jnp.concatenate([jnp.where(lane < LANES - 1, left[i], left[i + 1]) for i in pairs], axis=1),
        jnp.where(row > 0, pltpu.roll(x, 1, 0), south),
        jnp.where(row < rows - 1, pltpu.roll(x, rows - 1, 0), north),
    )


def stencil_kernel(
    tracer_ref, velocity_ref, mask_ref, fold_ref, a_ref, b_ref, *refs, carriers
):
    message_refs, out_ref = refs[:-1], refs[-1]
    channels, rows, columns = tracer_ref.shape
    levels = velocity_ref.shape[0] // 2
    lat = lax.axis_index("lat")
    lon = lax.axis_index("lon")
    odd = lat % 2 == 1
    at_top = lat == lax.axis_size("lat") - 1
    count = lax.axis_size("lon")
    edges = [ref[ref.shape[0] - rows :, :] for ref in message_refs]
    west, east = edges[0], edges[0]
    for k, edge in zip(carriers[1:], edges[1:]):
        partner = lax.bitwise_xor(lon, k)
        west = jnp.where(partner == (lon + count - 1) % count, edge, west)
        east = jnp.where(partner == (lon + 1) % count, edge, east)
    north = jnp.where(odd, a_ref[...], b_ref[...])
    south = jnp.where(odd, b_ref[...], a_ref[...])
    partner = fold_ref[...] - (count - 1 - lon) * columns
    pick = jnp.where(iota((columns, columns), 0) == partner, 1.0, 0.0).astype(BF16)
    high, rest = halves(north)
    middle, low = halves(rest)
    folded = sum(
        jnp.dot(x.astype(BF16), pick, preferred_element_type=F32) for x in (high, middle, low)
    )
    turn = jnp.where(iota(folded.shape, 0) // levels == channels // levels, -1.0, 1.0)
    north = jnp.where(at_top, folded * turn, north)

    def sides(x, lane, row):
        return shifted(
            x, west[:, lane : lane + 1], east[:, lane : lane + 1],
            south[row : row + 1], north[row : row + 1],
        )

    ocean = mask_ref[...].astype(F32)
    ocean_sides = sides(ocean, 2 * channels, channels + levels)
    opens = [ocean * side for side in ocean_sides]
    for level in range(levels):
        u = velocity_ref[level]
        v = velocity_ref[levels + level]
        u_w, u_e, _, _ = sides(u, channels + level, channels + level)
        _, _, v_s, v_n = sides(v, channels + level, channels + level)
        speeds = 0.25 * (u + u_w), 0.25 * (u + u_e), 0.25 * (v + v_s), 0.25 * (v + v_n)
        own, weights = 1.0, []
        for o, speed, sign in zip(opens, speeds, (1.0, -1.0, 1.0, -1.0)):
            near = o * (speed - sign * DIFFUSION)
            far = o * (speed + sign * DIFFUSION)
            own = own + sign * near
            weights.append(sign * far)
        for n in range(level, channels, levels):
            c = tracer_ref[n]
            total = own * c
            for weight, side in zip(weights, sides(c, n, n)):
                total = total + weight * side
            out_ref[n] = total


def scatter_kernel(*refs, messages, first, last, join, bound, shape):
    channels, rows, columns = shape
    slot_refs, refs = refs[:messages], refs[messages:]
    sum_ref, refs = (None, refs) if first else (refs[0], refs[1:])
    advected_ref, refs = (refs[0], refs[1:]) if join else (None, refs)
    out_ref, left_ref, hot_ref = refs
    pieces = bound // LANES
    base = pieces * channels
    bits = columns.bit_length() - 1
    slots = messages * bound
    for j, slot_ref in enumerate(slot_refs):
        for k in range(pieces):
            at = (j * pieces + k) * LANES
            here = slice(at, at + LANES)
            there = slice(slots + at, slots + at + LANES)
            spot = slot_ref[base + pieces + k : base + pieces + k + 1, :].astype(jnp.int32) - 1
            spot_row = lax.shift_right_arithmetic(spot, bits)
            spot_column = lax.bitwise_and(spot, columns - 1)
            hot = jnp.where(iota((columns, LANES), 0) == spot_column, 1.0, 0.0).astype(BF16)
            hot_ref[:, here] = hot
            hot_ref[:, there] = hot
            in_row = jnp.where(iota((rows, LANES), 0) == spot_row, 1.0, 0.0).astype(BF16)
            mass = slot_ref[k * channels : (k + 1) * channels, :]
            volume = slot_ref[base + k : base + k + 1, :]
            for x, top, n in ((mass, 0, channels), (volume, channels, 1)):
                for part, to in zip(halves(x), (here, there)):
                    for i in range(n):
                        spread = jnp.broadcast_to(part[i : i + 1], (16, LANES)).astype(BF16)
                        spread = jnp.concatenate([spread] * (rows // 16), axis=0)
                        left_ref[(top + i) * rows : (top + i + 1) * rows, to] = spread * in_row

    def summed(n, size):
        part = slice(n * rows, (n + size) * rows)
        new = lax.dot_general(left_ref[part, :], hot_ref[...], NT, preferred_element_type=F32)
        new = new if first else sum_ref[part, :] + new
        if join and n < channels:
            new = new + advected_ref[n : n + size].reshape(size * rows, columns)
        return new

    volume = summed(channels, 1)
    if last:
        scale = 1.0 / (1.0 + volume)
    else:
        out_ref[channels * rows :, :] = volume
    group = 8
    for n in range(0, channels, group):
        mass = summed(n, group)
        if last:
            for i in range(group):
                out_ref[n + i] = mass[i * rows : (i + 1) * rows] * scale
        else:
            out_ref[n * rows : (n + group) * rows, :] = mass


VMEM = pl.BlockSpec(memory_space=pltpu.VMEM)


HBM = pl.BlockSpec(memory_space=pltpu.MemorySpace.HBM)


def cost(microseconds):
    return pl.CostEstimate(flops=int(SCALE * microseconds), bytes_accessed=0, transcendentals=0)


def call(kernel, name, outs, *args, scratch=(), specs=None, aliases=None, cost=None):
    single = not isinstance(outs, (list, tuple))
    return pl.pallas_call(
        kernel,
        out_shape=outs,
        in_specs=specs or [VMEM] * len(args),
        out_specs=VMEM if single else [VMEM] * len(outs),
        scratch_shapes=list(scratch),
        input_output_aliases=aliases or {},
        compiler_params=pltpu.CompilerParams(vmem_limit_bytes=LIMIT),
        cost_estimate=cost,
        name=name,
    )(*args)


def SEQUENCE(count):
    far = list(range(count // 2, count - 1))
    near = [k for k in range(1, count // 2) if k & (k + 1)]
    carriers = [k for k in range(1, count // 2) if not k & (k + 1)]
    return ["b", "a", count - 1, far[0], *carriers, *far[1:], *near]


def GROUPS(sequence):
    keys = [k for k in sequence if k not in ("a", "b")]
    half = len(keys) // 2 + 1
    return [[0], keys[:half], keys[half:]], 2


def routes(lat_count, lon_count):
    first, second = [], []
    for lon in range(lon_count):
        for lat in range(lat_count):
            here = lon * lat_count + lat
            second.append((here, lon * lat_count + (lat ^ 1)))
            if lat == lat_count - 1:
                first.append((here, (lon_count - 1 - lon) * lat_count + lat))
            elif lat > 0:
                first.append((here, lon * lat_count + ((lat + 1) ^ 1) - 1))
    return first, second


def body(
    tracer, velocity, land_mask, fold_map, nested_tracer_field, nested_cell_volume, nest_parent
):
    tracers, levels, rows, columns = tracer.shape
    channels = tracers * levels
    lon_count, lat_count = lax.axis_size("lon"), lax.axis_size("lat")
    slot_count = nest_parent.shape[1]
    bound = 2 * slot_count // lon_count
    blocks = slot_count // LANES
    pieces = bound // LANES
    f32 = lambda *shape: jax.ShapeDtypeStruct(shape, F32)
    size = pieces * (channels + 2)
    carriers = [k for k in range(1, lon_count) if k & (k + 1) == 0]
    heights = [size + rows if k in carriers else size for k in range(lon_count)]
    c = tracer.reshape(channels, rows, columns)
    speed = velocity.reshape(2 * levels, rows, columns)
    line = f32(channels + levels + 8, columns)
    inputs = (
        nest_parent.reshape(blocks, LANES),
        nested_cell_volume.reshape(blocks, LANES),
        nested_tracer_field.reshape(channels * blocks, LANES),
        c, speed, land_mask,
    )
    results = call(
        lambda *refs: prepare_kernel(
            *refs, count=lon_count, bound=bound, cells=rows * columns, carriers=carriers
        ),
        "prepare",
        [f32(height, LANES) for height in heights] + [line, line],
        *[pltpu.with_memory_space_constraint(x, pltpu.MemorySpace.HBM) for x in inputs],
        specs=[HBM] * len(inputs),
        scratch=[pltpu.VMEM(x.shape, x.dtype) for x in inputs]
        + [
            pltpu.VMEM((lon_count * (2 * channels + 4), slot_count), BF16),
            pltpu.VMEM((bound, slot_count), BF16),
            pltpu.SemaphoreType.DMA((len(inputs),)),
        ],
    )
    buckets, (to_a, to_b) = results[:lon_count], results[lon_count:]
    arrived = {0: buckets[0]}
    first, second = routes(lat_count, lon_count)
    pair = lambda k: [(i, i ^ k) for i in range(lon_count)]
    sends = {k: (buckets[k], "lon", pair(k)) for k in range(1, lon_count)}
    sends["a"] = (to_a, ("lon", "lat"), first)
    sends["b"] = (to_b, ("lon", "lat"), second)
    sequence = SEQUENCE(lon_count)
    for n, key in enumerate(sequence):
        block, axes, pairs = sends[key]
        if n >= DEPTH:
            ahead = sequence[n - DEPTH]
            block, arrived[ahead] = lax.optimization_barrier((block, arrived[ahead]))
        arrived[key] = lax.ppermute(block, axes, pairs)
    grid = f32(channels, rows, columns)
    advected = call(
        lambda *refs: stencil_kernel(*refs, carriers=carriers),
        "stencil", grid, c, speed, land_mask, fold_map.reshape(1, columns),
        arrived["a"], arrived["b"], *[arrived[k] for k in carriers],
        cost=cost(3),
    )
    groups, joins = GROUPS(sequence)
    total = None
    for n, group in enumerate(groups):
        last = n == len(groups) - 1
        start = total is None
        join = n == joins
        args = [arrived[k] for k in group] + ([] if start else [total]) + ([advected] if join else [])
        total = call(
            lambda *refs: scatter_kernel(
                *refs, messages=len(group), first=start, last=last, join=join, bound=bound,
                shape=(channels, rows, columns),
            ),
            "scatter",
            grid if last else f32((channels + 1) * rows, columns),
            *args,
            aliases={} if start or last else {len(group): 0},
            scratch=[
                pltpu.VMEM(((channels + 1) * rows, 2 * len(group) * bound), BF16),
                pltpu.VMEM((columns, 2 * len(group) * bound), BF16),
            ],
            cost=cost(len(group)),
        )
    return total.reshape(tracer.shape)


def solution(mesh):
    in_specs = (
        P(None, None, "lat", "lon"),
        P(None, None, "lat", "lon"),
        P("lat", "lon"),
        P("lon"),
        P(None, None, "lat", "lon"),
        P("lat", "lon"),
        P("lat", "lon"),
    )
    out_specs = P(None, None, "lat", "lon")
    return jax.shard_map(body, mesh=mesh, in_specs=in_specs, out_specs=out_specs, check_vma=False)
```

```python
import jax
import jax.numpy as jnp
from jax import lax
from jax.experimental import pallas as pl
from jax.experimental.pallas import tpu as pltpu
from jax.sharding import PartitionSpec as P

DIFFUSION = 0.15
LANES = 128
LIMIT = 32 << 20
SCALE = 1e9
DEPTH = 5
CUTS = (17,)
F32 = jnp.float32
BF16 = jnp.bfloat16
NT = (((1,), (1,)), ((), ()))


def halves(x):
    high = x.astype(BF16).astype(F32)
    return high, x - high


def iota(shape, dim):
    return lax.broadcasted_iota(jnp.int32, shape, dim)


def prepare_kernel(*refs, count, bound, cells, carriers):
    sources, out_refs, edge_refs = refs[:6], refs[6 : 6 + count], refs[6 + count : 8 + count]
    held, (left_ref, hot_ref, sems) = refs[8 + count : 14 + count], refs[14 + count :]
    copies = [
        pltpu.make_async_copy(source, ref, sems.at[n])
        for n, (source, ref) in enumerate(zip(sources, held))
    ]
    for copy in copies:
        copy.start()
    copies[0].wait()
    parent_ref, volume_ref, field_ref, *grid_refs = held
    blocks = parent_ref.shape[0]
    channels = field_ref.shape[0] // blocks
    shift = cells.bit_length() - 1
    parent = parent_ref[...]
    me = lax.axis_index("lon")
    owner = lax.bitwise_xor(lax.shift_right_arithmetic(parent, shift), me)
    owner = jnp.where(parent >= 0, owner, -1)
    inside = (lax.bitwise_and(parent, cells - 1) + 1).astype(F32)
    member = jnp.concatenate([jnp.where(owner == d, 1.0, 0.0) for d in range(count)], axis=0)
    square = (LANES, LANES)
    before = jnp.where(iota(square, 0) < iota(square, 1), 1.0, 0.0).astype(BF16)
    within = jnp.dot(member.astype(BF16), before, preferred_element_type=F32)
    total = jnp.broadcast_to(jnp.sum(member, axis=1, keepdims=True), member.shape)
    rows = count * blocks
    one, two = iota((rows, rows), 0), iota((rows, rows), 1)
    bits = blocks.bit_length() - 1
    same = lax.shift_right_logical(one, bits) == lax.shift_right_logical(two, bits)
    earlier = jnp.where(same & (two < one), 1.0, 0.0).astype(BF16)
    place = within + jnp.dot(earlier, total.astype(BF16), preferred_element_type=F32)
    picked = place * member
    rank = picked[:blocks]
    for d in range(1, count):
        rank = rank + picked[d * blocks : (d + 1) * blocks]
    rank = jnp.where(parent >= 0, rank, -1.0).astype(jnp.int32)
    extra = count * 2 * channels
    copies[1].wait()
    copies[2].wait()
    for b in range(blocks):
        lanes = slice(b * LANES, (b + 1) * LANES)
        spots = iota((bound, LANES), 0)
        hot_ref[:, lanes] = jnp.where(spots == rank[b : b + 1], 1.0, 0.0).astype(BF16)
        volume = volume_ref[b : b + 1, :]
        mass = field_ref[pl.ds(b, channels, stride=blocks), :] * volume
        pair = jnp.concatenate(halves(mass), axis=0)
        mine = [member[d * blocks + b : d * blocks + b + 1] for d in range(count)]
        for d in range(count):
            left_ref[d * 2 * channels : (d + 1) * 2 * channels, lanes] = (pair * mine[d]).astype(BF16)
        mask = jnp.concatenate(mine, axis=0)
        small = [h * mask for x in (volume, inside[b : b + 1]) for h in halves(x)]
        left_ref[extra : extra + 4 * count, lanes] = jnp.concatenate(small, axis=0).astype(BF16)
    result = lax.dot_general(left_ref[...], hot_ref[...], NT, preferred_element_type=F32)
    pieces = bound // LANES
    volumes = result[extra : extra + count] + result[extra + count : extra + 2 * count]
    insides = (
        result[extra + 2 * count : extra + 3 * count] + result[extra + 3 * count : extra + 4 * count]
    )
    base = pieces * channels
    for d in range(count):
        top = d * 2 * channels
        mass = result[top : top + channels] + result[top + channels : top + 2 * channels]
        for k in range(pieces):
            lanes = slice(k * LANES, (k + 1) * LANES)
            out_refs[d][k * channels : (k + 1) * channels, :] = mass[:, lanes]
            out_refs[d][base + k : base + k + 1, :] = volumes[d : d + 1, lanes]
            out_refs[d][base + pieces + k : base + pieces + k + 1, :] = insides[d : d + 1, lanes]
    for copy in copies[3:]:
        copy.wait()
    pack_edges(*grid_refs, {k: out_refs[k] for k in carriers}, *edge_refs, count)


def pack_edges(tracer_ref, velocity_ref, mask_ref, message_refs, a_ref, b_ref, count):
    channels, rows, columns = tracer_ref.shape
    levels = velocity_ref.shape[0] // 2
    ocean = mask_ref[...].astype(F32)
    lane = iota((rows, LANES), 1)
    edges = []
    for at in (0, columns - 1):
        edge = slice(at, at + 1)
        packed = jnp.where(lane < 3 * channels, ocean[:, edge], 0.0)
        for n in range(levels):
            spot = (lane >= channels) & (lane < 2 * channels) & (lane % levels == n)
            packed = jnp.where(spot, velocity_ref[n, :, edge], packed)
        for n in range(channels):
            packed = jnp.where(lane == n, tracer_ref[n, :, edge], packed)
        edges.append(packed)
    me = lax.axis_index("lon")
    for k, ref in message_refs.items():
        is_west = lax.bitwise_xor(me, k) == (me + count - 1) % count
        ref[ref.shape[0] - rows :, :] = jnp.where(is_west, edges[0], edges[1])
    odd = lax.axis_index("lat") % 2 == 1
    for top, n, ref in ((0, channels, tracer_ref), (channels, levels, velocity_ref)):
        start = 0 if top == 0 else levels
        first = ref[start : start + n, 0, :]
        last = ref[start : start + n, rows - 1, :]
        a_ref[top : top + n, :] = jnp.where(odd, last, first)
        b_ref[top : top + n, :] = jnp.where(odd, first, last)
    first = jnp.broadcast_to(ocean[0:1], (8, columns))
    last = jnp.broadcast_to(ocean[rows - 1 : rows], (8, columns))
    top = channels + levels
    a_ref[top : top + 8, :] = jnp.where(odd, last, first)
    b_ref[top : top + 8, :] = jnp.where(odd, first, last)


def shifted(x, west, east, south, north):
    rows, columns = x.shape
    lane = iota((rows, LANES), 1)
    row = iota((rows, columns), 0)
    tiles = [x[:, at : at + LANES] for at in range(0, columns, LANES)]
    left = [pltpu.roll(t, LANES - 1, 1) for t in tiles] + [east]
    right = [west] + [pltpu.roll(t, 1, 1) for t in tiles]
    pairs = range(len(tiles))
    return (
        jnp.concatenate([jnp.where(lane > 0, right[i + 1], right[i]) for i in pairs], axis=1),
        jnp.concatenate([jnp.where(lane < LANES - 1, left[i], left[i + 1]) for i in pairs], axis=1),
        jnp.where(row > 0, pltpu.roll(x, 1, 0), south),
        jnp.where(row < rows - 1, pltpu.roll(x, rows - 1, 0), north),
    )


def stencil_kernel(
    tracer_ref, velocity_ref, mask_ref, fold_ref, a_ref, b_ref, *refs, carriers
):
    message_refs, out_ref = refs[:-1], refs[-1]
    channels, rows, columns = tracer_ref.shape
    levels = velocity_ref.shape[0] // 2
    lat = lax.axis_index("lat")
    lon = lax.axis_index("lon")
    odd = lat % 2 == 1
    at_top = lat == lax.axis_size("lat") - 1
    count = lax.axis_size("lon")
    edges = [ref[ref.shape[0] - rows :, :] for ref in message_refs]
    west, east = edges[0], edges[0]
    for k, edge in zip(carriers[1:], edges[1:]):
        partner = lax.bitwise_xor(lon, k)
        west = jnp.where(partner == (lon + count - 1) % count, edge, west)
        east = jnp.where(partner == (lon + 1) % count, edge, east)
    north = jnp.where(odd, a_ref[...], b_ref[...])
    south = jnp.where(odd, b_ref[...], a_ref[...])
    partner = fold_ref[...] - (count - 1 - lon) * columns
    pick = jnp.where(iota((columns, columns), 0) == partner, 1.0, 0.0).astype(BF16)
    high, rest = halves(north)
    parts = jnp.concatenate([high, *halves(rest)], axis=0).astype(BF16)
    folded = jnp.dot(parts, pick, preferred_element_type=F32)
    height = north.shape[0]
    folded = folded[:height] + folded[height : 2 * height] + folded[2 * height :]
    turn = jnp.where(iota(folded.shape, 0) // levels == channels // levels, -1.0, 1.0)
    north = jnp.where(at_top, folded * turn, north)

    def sides(x, lane, row):
        return shifted(
            x, west[:, lane : lane + 1], east[:, lane : lane + 1],
            south[row : row + 1], north[row : row + 1],
        )

    ocean = mask_ref[...].astype(F32)
    ocean_sides = sides(ocean, 2 * channels, channels + levels)
    opens = [ocean * side for side in ocean_sides]
    for level in range(levels):
        u = velocity_ref[level]
        v = velocity_ref[levels + level]
        u_w, u_e, _, _ = sides(u, channels + level, channels + level)
        _, _, v_s, v_n = sides(v, channels + level, channels + level)
        speeds = 0.25 * (u + u_w), 0.25 * (u + u_e), 0.25 * (v + v_s), 0.25 * (v + v_n)
        own, weights = 1.0, []
        for o, speed, sign in zip(opens, speeds, (1.0, -1.0, 1.0, -1.0)):
            near = o * (speed - sign * DIFFUSION)
            far = o * (speed + sign * DIFFUSION)
            own = own + sign * near
            weights.append(sign * far)
        for n in range(level, channels, levels):
            c = tracer_ref[n]
            total = own * c
            for weight, side in zip(weights, sides(c, n, n)):
                total = total + weight * side
            out_ref[n] = total


def expand(slot_refs, left_ref, hot_ref, *, bound, shape):
    channels, rows, columns = shape
    pieces = bound // LANES
    base = pieces * channels
    bits = columns.bit_length() - 1
    slots = len(slot_refs) * bound
    for j, slot_ref in enumerate(slot_refs):
        for k in range(pieces):
            at = (j * pieces + k) * LANES
            here = slice(at, at + LANES)
            there = slice(slots + at, slots + at + LANES)
            spot = slot_ref[base + pieces + k : base + pieces + k + 1, :].astype(jnp.int32) - 1
            spot_row = lax.shift_right_arithmetic(spot, bits)
            spot_column = lax.bitwise_and(spot, columns - 1)
            hot = jnp.where(iota((columns, LANES), 0) == spot_column, 1.0, 0.0).astype(BF16)
            hot_ref[:, here] = hot
            hot_ref[:, there] = hot
            in_row = jnp.where(iota((rows, LANES), 0) == spot_row, 1.0, 0.0).astype(BF16)
            mass = slot_ref[k * channels : (k + 1) * channels, :]
            volume = slot_ref[base + k : base + k + 1, :]
            for x, top, n in ((volume, 0, 1), (mass, 1, channels)):
                for part, to in zip(halves(x), (here, there)):
                    for i in range(n):
                        spread = jnp.broadcast_to(part[i : i + 1], (16, LANES)).astype(BF16)
                        spread = jnp.concatenate([spread] * (rows // 16), axis=0)
                        left_ref[(top + i) * rows : (top + i + 1) * rows, to] = spread * in_row


def scatter_kernel(*refs, messages, bound, shape):
    slot_refs, (*sum_refs, out_ref, left_ref, hot_ref) = refs[:messages], refs[messages:]
    expand(slot_refs, left_ref, hot_ref, bound=bound, shape=shape)
    new = lax.dot_general(left_ref[...], hot_ref[...], NT, preferred_element_type=F32)
    for ref in sum_refs:
        new = new + ref[...]
    out_ref[...] = new


def final_kernel(*refs, messages, bound, shape):
    channels, rows, columns = shape
    slot_refs, refs = refs[:messages], refs[messages:]
    sum_ref, advected_ref, out_ref, left_ref, hot_ref, held_ref, sems = refs
    expand(slot_refs, left_ref, hot_ref, bound=bound, shape=shape)
    copies, scale = [], None
    cuts = CUTS
    for start, stop in zip((0,) + cuts, cuts + (channels + 1,)):
        part = slice(start * rows, stop * rows)
        new = lax.dot_general(left_ref[part, :], hot_ref[...], NT, preferred_element_type=F32)
        new = new + sum_ref[part, :]
        if start == 0:
            scale = 1.0 / (1.0 + new[:rows])
        for n in range(max(start, 1), stop):
            mass = new[(n - start) * rows : (n - start + 1) * rows]
            held_ref[n - 1] = (advected_ref[n - 1] + mass) * scale
        done = slice(max(start, 1) - 1, stop - 1)
        copies.append(
            pltpu.make_async_copy(held_ref.at[done], out_ref.at[done], sems.at[len(copies)])
        )
        copies[-1].start()
    for copy in copies:
        copy.wait()


VMEM = pl.BlockSpec(memory_space=pltpu.VMEM)


HBM = pl.BlockSpec(memory_space=pltpu.MemorySpace.HBM)


def cost(microseconds):
    return pl.CostEstimate(flops=int(SCALE * microseconds), bytes_accessed=0, transcendentals=0)


def call(kernel, name, outs, *args, scratch=(), specs=None, out_specs=None, cost=None):
    single = not isinstance(outs, (list, tuple))
    return pl.pallas_call(
        kernel,
        out_shape=outs,
        in_specs=specs or [VMEM] * len(args),
        out_specs=out_specs or (VMEM if single else [VMEM] * len(outs)),
        scratch_shapes=list(scratch),
        compiler_params=pltpu.CompilerParams(vmem_limit_bytes=LIMIT),
        cost_estimate=cost,
        name=name,
    )(*args)


def PLAN(count):
    far = list(range(count // 2, count - 1))
    near = [k for k in range(1, count // 2) if k & (k + 1)]
    carriers = [k for k in range(1, count // 2) if not k & (k + 1)][::-1]
    keys = ["b", "a", count - 1, far[0], *carriers, *far[1:], *near]
    sequence = [(key, keys[n - DEPTH] if n >= DEPTH else None) for n, key in enumerate(keys)]
    cut = 4 + len(carriers)
    return sequence, [[0], keys[2:cut], keys[cut : cut + 1], keys[cut + 1 :]]


def routes(lat_count, lon_count):
    first, second = [], []
    for lon in range(lon_count):
        for lat in range(lat_count):
            here = lon * lat_count + lat
            second.append((here, lon * lat_count + (lat ^ 1)))
            if lat == lat_count - 1:
                first.append((here, (lon_count - 1 - lon) * lat_count + lat))
            elif lat > 0:
                first.append((here, lon * lat_count + ((lat + 1) ^ 1) - 1))
    return first, second


def body(
    tracer, velocity, land_mask, fold_map, nested_tracer_field, nested_cell_volume, nest_parent
):
    tracers, levels, rows, columns = tracer.shape
    channels = tracers * levels
    lon_count, lat_count = lax.axis_size("lon"), lax.axis_size("lat")
    slot_count = nest_parent.shape[1]
    bound = 2 * slot_count // lon_count
    blocks = slot_count // LANES
    pieces = bound // LANES
    f32 = lambda *shape: jax.ShapeDtypeStruct(shape, F32)
    size = pieces * (channels + 2)
    carriers = [k for k in range(1, lon_count) if k & (k + 1) == 0]
    heights = [size + rows if k in carriers else size for k in range(lon_count)]
    c = tracer.reshape(channels, rows, columns)
    speed = velocity.reshape(2 * levels, rows, columns)
    line = f32(channels + levels + 8, columns)
    inputs = (
        nest_parent.reshape(blocks, LANES),
        nested_cell_volume.reshape(blocks, LANES),
        nested_tracer_field.reshape(channels * blocks, LANES),
        c, speed, land_mask,
    )
    results = call(
        lambda *refs: prepare_kernel(
            *refs, count=lon_count, bound=bound, cells=rows * columns, carriers=carriers
        ),
        "prepare",
        [f32(height, LANES) for height in heights] + [line, line],
        *[pltpu.with_memory_space_constraint(x, pltpu.MemorySpace.HBM) for x in inputs],
        specs=[HBM] * len(inputs),
        scratch=[pltpu.VMEM(x.shape, x.dtype) for x in inputs]
        + [
            pltpu.VMEM((lon_count * (2 * channels + 4), slot_count), BF16),
            pltpu.VMEM((bound, slot_count), BF16),
            pltpu.SemaphoreType.DMA((len(inputs),)),
        ],
    )
    buckets, (to_a, to_b) = results[:lon_count], results[lon_count:]
    arrived = {0: buckets[0]}
    first, second = routes(lat_count, lon_count)
    pair = lambda k: [(i, i ^ k) for i in range(lon_count)]
    sends = {k: (buckets[k], "lon", pair(k)) for k in range(1, lon_count)}
    sends["a"] = (to_a, ("lon", "lat"), first)
    sends["b"] = (to_b, ("lon", "lat"), second)
    sequence, groups = PLAN(lon_count)
    for key, ahead in sequence:
        block, axes, pairs = sends[key]
        if ahead is not None:
            block, arrived[ahead] = lax.optimization_barrier((block, arrived[ahead]))
        arrived[key] = lax.ppermute(block, axes, pairs)
    shape = (channels, rows, columns)
    size_of = lambda group: [
        pltpu.VMEM(((channels + 1) * rows, 2 * len(group) * bound), BF16),
        pltpu.VMEM((columns, 2 * len(group) * bound), BF16),
    ]
    advected = call(
        lambda *refs: stencil_kernel(*refs, carriers=carriers),
        "stencil", f32(*shape), c, speed, land_mask, fold_map.reshape(1, columns),
        arrived["a"], arrived["b"], *[arrived[k] for k in carriers],
        cost=cost(1.5),
    )
    sums = []
    for group in groups[:-1]:
        sums = [
            call(
                lambda *refs: scatter_kernel(*refs, messages=len(group), bound=bound, shape=shape),
                "scatter",
                f32((channels + 1) * rows, columns),
                *[arrived[k] for k in group],
                *sums,
                scratch=size_of(group),
                cost=cost(len(group)),
            )
        ]
    group = groups[-1]
    after = call(
        lambda *refs: final_kernel(
            *refs, messages=len(group), bound=bound, shape=shape
        ),
        "final",
        f32(*shape),
        *[arrived[k] for k in group],
        *sums,
        advected,
        scratch=size_of(group) + [pltpu.VMEM(shape, F32), pltpu.SemaphoreType.DMA((len(CUTS) + 1,))],
        out_specs=HBM,
        cost=cost(len(group)),
    )
    return after.reshape(tracer.shape)


def solution(mesh):
    in_specs = (
        P(None, None, "lat", "lon"),
        P(None, None, "lat", "lon"),
        P("lat", "lon"),
        P("lon"),
        P(None, None, "lat", "lon"),
        P("lat", "lon"),
        P("lat", "lon"),
    )
    out_specs = P(None, None, "lat", "lon")
    return jax.shard_map(body, mesh=mesh, in_specs=in_specs, out_specs=out_specs, check_vma=False)
```

```python
import jax
import jax.numpy as jnp
from jax import lax
from jax.experimental import pallas as pl
from jax.experimental.pallas import tpu as pltpu
from jax.sharding import PartitionSpec as P

DIFFUSION = 0.15
LANES = 128
LIMIT = 32 << 20
SCALE = 1e9
DEPTH = 5
CUTS = ()
F32 = jnp.float32
BF16 = jnp.bfloat16
NT = (((1,), (1,)), ((), ()))


def halves(x):
    high = x.astype(BF16).astype(F32)
    return high, x - high


def iota(shape, dim):
    return lax.broadcasted_iota(jnp.int32, shape, dim)


def prepare_kernel(*refs, count, bound, cells, carriers):
    sources, out_refs, edge_refs = refs[:6], refs[6 : 6 + count], refs[6 + count : 8 + count]
    held, (left_ref, hot_ref, sems) = refs[8 + count : 14 + count], refs[14 + count :]
    copies = [
        pltpu.make_async_copy(source, ref, sems.at[n])
        for n, (source, ref) in enumerate(zip(sources, held))
    ]
    for copy in copies:
        copy.start()
    copies[0].wait()
    parent_ref, volume_ref, field_ref, *grid_refs = held
    blocks = parent_ref.shape[0]
    channels = field_ref.shape[0] // blocks
    shift = cells.bit_length() - 1
    parent = parent_ref[...]
    me = lax.axis_index("lon")
    owner = lax.bitwise_xor(lax.shift_right_arithmetic(parent, shift), me)
    owner = jnp.where(parent >= 0, owner, -1)
    inside = (lax.bitwise_and(parent, cells - 1) + 1).astype(F32)
    member = jnp.concatenate([jnp.where(owner == d, 1.0, 0.0) for d in range(count)], axis=0)
    square = (LANES, LANES)
    before = jnp.where(iota(square, 0) < iota(square, 1), 1.0, 0.0).astype(BF16)
    within = jnp.dot(member.astype(BF16), before, preferred_element_type=F32)
    total = jnp.broadcast_to(jnp.sum(member, axis=1, keepdims=True), member.shape)
    rows = count * blocks
    one, two = iota((rows, rows), 0), iota((rows, rows), 1)
    bits = blocks.bit_length() - 1
    same = lax.shift_right_logical(one, bits) == lax.shift_right_logical(two, bits)
    earlier = jnp.where(same & (two < one), 1.0, 0.0).astype(BF16)
    place = within + jnp.dot(earlier, total.astype(BF16), preferred_element_type=F32)
    picked = place * member
    rank = picked[:blocks]
    for d in range(1, count):
        rank = rank + picked[d * blocks : (d + 1) * blocks]
    rank = jnp.where(parent >= 0, rank, -1.0).astype(jnp.int32)
    extra = count * 2 * channels
    copies[1].wait()
    copies[2].wait()
    for b in range(blocks):
        lanes = slice(b * LANES, (b + 1) * LANES)
        spots = iota((bound, LANES), 0)
        hot_ref[:, lanes] = jnp.where(spots == rank[b : b + 1], 1.0, 0.0).astype(BF16)
        volume = volume_ref[b : b + 1, :]
        mass = field_ref[pl.ds(b, channels, stride=blocks), :] * volume
        pair = jnp.concatenate(halves(mass), axis=0).astype(BF16)
        mine = [member[d * blocks + b : d * blocks + b + 1] for d in range(count)]
        for d in range(count):
            chosen = jnp.broadcast_to(mine[d], (16, LANES)).astype(BF16)
            chosen = jnp.concatenate([chosen] * (2 * channels // 16), axis=0)
            left_ref[d * 2 * channels : (d + 1) * 2 * channels, lanes] = pair * chosen
        mask = jnp.concatenate(mine, axis=0)
        small = [h * mask for x in (volume, inside[b : b + 1]) for h in halves(x)]
        left_ref[extra : extra + 4 * count, lanes] = jnp.concatenate(small, axis=0).astype(BF16)
    result = lax.dot_general(left_ref[...], hot_ref[...], NT, preferred_element_type=F32)
    pieces = bound // LANES
    volumes = result[extra : extra + count] + result[extra + count : extra + 2 * count]
    insides = (
        result[extra + 2 * count : extra + 3 * count] + result[extra + 3 * count : extra + 4 * count]
    )
    base = pieces * channels
    for d in range(count):
        top = d * 2 * channels
        mass = result[top : top + channels] + result[top + channels : top + 2 * channels]
        for k in range(pieces):
            lanes = slice(k * LANES, (k + 1) * LANES)
            out_refs[d][k * channels : (k + 1) * channels, :] = mass[:, lanes]
            out_refs[d][base + k : base + k + 1, :] = volumes[d : d + 1, lanes]
            out_refs[d][base + pieces + k : base + pieces + k + 1, :] = insides[d : d + 1, lanes]
    for copy in copies[3:]:
        copy.wait()
    pack_edges(*grid_refs, {k: out_refs[k] for k in carriers}, *edge_refs, count)


def pack_edges(tracer_ref, velocity_ref, mask_ref, message_refs, a_ref, b_ref, count):
    channels, rows, columns = tracer_ref.shape
    levels = velocity_ref.shape[0] // 2
    ocean = mask_ref[...].astype(F32)
    lane = iota((rows, LANES), 1)
    edges = []
    for at in (0, columns - 1):
        edge = slice(at, at + 1)
        packed = jnp.where(lane < 3 * channels, ocean[:, edge], 0.0)
        for n in range(levels):
            spot = (lane >= channels) & (lane < 2 * channels) & (lane % levels == n)
            packed = jnp.where(spot, velocity_ref[n, :, edge], packed)
        for n in range(channels):
            packed = jnp.where(lane == n, tracer_ref[n, :, edge], packed)
        edges.append(packed)
    me = lax.axis_index("lon")
    for k, ref in message_refs.items():
        is_west = lax.bitwise_xor(me, k) == (me + count - 1) % count
        ref[ref.shape[0] - rows :, :] = jnp.where(is_west, edges[0], edges[1])
    odd = lax.axis_index("lat") % 2 == 1
    for top, n, ref in ((0, channels, tracer_ref), (channels, levels, velocity_ref)):
        start = 0 if top == 0 else levels
        first = ref[start : start + n, 0, :]
        last = ref[start : start + n, rows - 1, :]
        a_ref[top : top + n, :] = jnp.where(odd, last, first)
        b_ref[top : top + n, :] = jnp.where(odd, first, last)
    first = jnp.broadcast_to(ocean[0:1], (8, columns))
    last = jnp.broadcast_to(ocean[rows - 1 : rows], (8, columns))
    top = channels + levels
    a_ref[top : top + 8, :] = jnp.where(odd, last, first)
    b_ref[top : top + 8, :] = jnp.where(odd, first, last)


def shifted(x, west, east, south, north):
    rows, columns = x.shape
    lane = iota((rows, LANES), 1)
    row = iota((rows, columns), 0)
    tiles = [x[:, at : at + LANES] for at in range(0, columns, LANES)]
    left = [pltpu.roll(t, LANES - 1, 1) for t in tiles] + [east]
    right = [west] + [pltpu.roll(t, 1, 1) for t in tiles]
    pairs = range(len(tiles))
    return (
        jnp.concatenate([jnp.where(lane > 0, right[i + 1], right[i]) for i in pairs], axis=1),
        jnp.concatenate([jnp.where(lane < LANES - 1, left[i], left[i + 1]) for i in pairs], axis=1),
        jnp.where(row > 0, pltpu.roll(x, 1, 0), south),
        jnp.where(row < rows - 1, pltpu.roll(x, rows - 1, 0), north),
    )


def stencil_kernel(
    tracer_ref, velocity_ref, mask_ref, fold_ref, a_ref, b_ref, *refs, carriers
):
    message_refs, out_ref = refs[:-1], refs[-1]
    channels, rows, columns = tracer_ref.shape
    levels = velocity_ref.shape[0] // 2
    lat = lax.axis_index("lat")
    lon = lax.axis_index("lon")
    odd = lat % 2 == 1
    at_top = lat == lax.axis_size("lat") - 1
    count = lax.axis_size("lon")
    edges = [ref[ref.shape[0] - rows :, :] for ref in message_refs]
    west, east = edges[0], edges[0]
    for k, edge in zip(carriers[1:], edges[1:]):
        partner = lax.bitwise_xor(lon, k)
        west = jnp.where(partner == (lon + count - 1) % count, edge, west)
        east = jnp.where(partner == (lon + 1) % count, edge, east)
    north = jnp.where(odd, a_ref[...], b_ref[...])
    south = jnp.where(odd, b_ref[...], a_ref[...])
    partner = fold_ref[...] - (count - 1 - lon) * columns
    pick = jnp.where(iota((columns, columns), 0) == partner, 1.0, 0.0).astype(BF16)
    high, rest = halves(north)
    parts = jnp.concatenate([high, *halves(rest)], axis=0).astype(BF16)
    folded = jnp.dot(parts, pick, preferred_element_type=F32)
    height = north.shape[0]
    folded = folded[:height] + folded[height : 2 * height] + folded[2 * height :]
    turn = jnp.where(iota(folded.shape, 0) // levels == channels // levels, -1.0, 1.0)
    north = jnp.where(at_top, folded * turn, north)

    def sides(x, lane, row):
        return shifted(
            x, west[:, lane : lane + 1], east[:, lane : lane + 1],
            south[row : row + 1], north[row : row + 1],
        )

    ocean = mask_ref[...].astype(F32)
    ocean_sides = sides(ocean, 2 * channels, channels + levels)
    opens = [ocean * side for side in ocean_sides]
    for level in range(levels):
        u = velocity_ref[level]
        v = velocity_ref[levels + level]
        u_w, u_e, _, _ = sides(u, channels + level, channels + level)
        _, _, v_s, v_n = sides(v, channels + level, channels + level)
        speeds = 0.25 * (u + u_w), 0.25 * (u + u_e), 0.25 * (v + v_s), 0.25 * (v + v_n)
        own, weights = 1.0, []
        for o, speed, sign in zip(opens, speeds, (1.0, -1.0, 1.0, -1.0)):
            near = o * (speed - sign * DIFFUSION)
            far = o * (speed + sign * DIFFUSION)
            own = own + sign * near
            weights.append(sign * far)
        for n in range(level, channels, levels):
            c = tracer_ref[n]
            total = own * c
            for weight, side in zip(weights, sides(c, n, n)):
                total = total + weight * side
            out_ref[n] = total


def expand(slot_refs, left_ref, hot_ref, *, bound, shape):
    channels, rows, columns = shape
    pieces = bound // LANES
    base = pieces * channels
    bits = columns.bit_length() - 1
    slots = len(slot_refs) * bound
    for j, slot_ref in enumerate(slot_refs):
        for k in range(pieces):
            at = (j * pieces + k) * LANES
            here = slice(at, at + LANES)
            there = slice(slots + at, slots + at + LANES)
            spot = slot_ref[base + pieces + k : base + pieces + k + 1, :].astype(jnp.int32) - 1
            spot_row = lax.shift_right_arithmetic(spot, bits)
            spot_column = lax.bitwise_and(spot, columns - 1)
            hot = jnp.where(iota((columns, LANES), 0) == spot_column, 1.0, 0.0).astype(BF16)
            hot_ref[:, here] = hot
            hot_ref[:, there] = hot
            in_row = jnp.where(iota((rows, LANES), 0) == spot_row, 1.0, 0.0).astype(BF16)
            mass = slot_ref[k * channels : (k + 1) * channels, :]
            volume = slot_ref[base + k : base + k + 1, :]
            for x, top, n in ((volume, 0, 1), (mass, 1, channels)):
                for part, to in zip(halves(x), (here, there)):
                    for i in range(n):
                        spread = jnp.broadcast_to(part[i : i + 1], (16, LANES)).astype(BF16)
                        spread = jnp.concatenate([spread] * (rows // 16), axis=0)
                        left_ref[(top + i) * rows : (top + i + 1) * rows, to] = spread * in_row


def scatter_kernel(*refs, messages, bound, shape):
    slot_refs, (*sum_refs, out_ref, left_ref, hot_ref) = refs[:messages], refs[messages:]
    expand(slot_refs, left_ref, hot_ref, bound=bound, shape=shape)
    new = lax.dot_general(left_ref[...], hot_ref[...], NT, preferred_element_type=F32)
    for ref in sum_refs:
        new = new + ref[...]
    out_ref[...] = new


def final_kernel(*refs, messages, bound, shape):
    channels, rows, columns = shape
    slot_refs, refs = refs[:messages], refs[messages:]
    sum_ref, advected_ref, out_ref, left_ref, hot_ref, held_ref, sems = refs
    expand(slot_refs, left_ref, hot_ref, bound=bound, shape=shape)
    copies, scale = [], None
    cuts = CUTS
    for start, stop in zip((0,) + cuts, cuts + (channels + 1,)):
        part = slice(start * rows, stop * rows)
        new = lax.dot_general(left_ref[part, :], hot_ref[...], NT, preferred_element_type=F32)
        new = new + sum_ref[part, :]
        if start == 0:
            scale = 1.0 / (1.0 + new[:rows])
        for n in range(max(start, 1), stop):
            mass = new[(n - start) * rows : (n - start + 1) * rows]
            held_ref[n - 1] = (advected_ref[n - 1] + mass) * scale
        done = slice(max(start, 1) - 1, stop - 1)
        copies.append(
            pltpu.make_async_copy(held_ref.at[done], out_ref.at[done], sems.at[len(copies)])
        )
        copies[-1].start()
    for copy in copies:
        copy.wait()


VMEM = pl.BlockSpec(memory_space=pltpu.VMEM)


HBM = pl.BlockSpec(memory_space=pltpu.MemorySpace.HBM)


def cost(microseconds):
    return pl.CostEstimate(flops=int(SCALE * microseconds), bytes_accessed=0, transcendentals=0)


def call(kernel, name, outs, *args, scratch=(), specs=None, out_specs=None, cost=None):
    single = not isinstance(outs, (list, tuple))
    return pl.pallas_call(
        kernel,
        out_shape=outs,
        in_specs=specs or [VMEM] * len(args),
        out_specs=out_specs or (VMEM if single else [VMEM] * len(outs)),
        scratch_shapes=list(scratch),
        compiler_params=pltpu.CompilerParams(vmem_limit_bytes=LIMIT),
        cost_estimate=cost,
        name=name,
    )(*args)


def PLAN(count):
    far = list(range(count // 2, count - 1))
    near = [k for k in range(1, count // 2) if k & (k + 1)]
    carriers = [k for k in range(1, count // 2) if not k & (k + 1)][::-1]
    keys = ["b", "a", count - 1, far[0], *carriers, *far[1:], *near]
    sequence = [(key, keys[n - DEPTH] if n >= DEPTH else None) for n, key in enumerate(keys)]
    cut = 4 + len(carriers)
    return sequence, [[0], keys[2:cut], keys[cut : cut + 1], keys[cut + 1 :]]


def routes(lat_count, lon_count):
    first, second = [], []
    for lon in range(lon_count):
        for lat in range(lat_count):
            here = lon * lat_count + lat
            second.append((here, lon * lat_count + (lat ^ 1)))
            if lat == lat_count - 1:
                first.append((here, (lon_count - 1 - lon) * lat_count + lat))
            elif lat > 0:
                first.append((here, lon * lat_count + ((lat + 1) ^ 1) - 1))
    return first, second


def body(
    tracer, velocity, land_mask, fold_map, nested_tracer_field, nested_cell_volume, nest_parent
):
    tracers, levels, rows, columns = tracer.shape
    channels = tracers * levels
    lon_count, lat_count = lax.axis_size("lon"), lax.axis_size("lat")
    slot_count = nest_parent.shape[1]
    bound = 2 * slot_count // lon_count
    blocks = slot_count // LANES
    pieces = bound // LANES
    f32 = lambda *shape: jax.ShapeDtypeStruct(shape, F32)
    size = pieces * (channels + 2)
    carriers = [k for k in range(1, lon_count) if k & (k + 1) == 0]
    heights = [size + rows if k in carriers else size for k in range(lon_count)]
    c = tracer.reshape(channels, rows, columns)
    speed = velocity.reshape(2 * levels, rows, columns)
    line = f32(channels + levels + 8, columns)
    inputs = (
        nest_parent.reshape(blocks, LANES),
        nested_cell_volume.reshape(blocks, LANES),
        nested_tracer_field.reshape(channels * blocks, LANES),
        c, speed, land_mask,
    )
    results = call(
        lambda *refs: prepare_kernel(
            *refs, count=lon_count, bound=bound, cells=rows * columns, carriers=carriers
        ),
        "prepare",
        [f32(height, LANES) for height in heights] + [line, line],
        *[pltpu.with_memory_space_constraint(x, pltpu.MemorySpace.HBM) for x in inputs],
        specs=[HBM] * len(inputs),
        scratch=[pltpu.VMEM(x.shape, x.dtype) for x in inputs]
        + [
            pltpu.VMEM((lon_count * (2 * channels + 4), slot_count), BF16),
            pltpu.VMEM((bound, slot_count), BF16),
            pltpu.SemaphoreType.DMA((len(inputs),)),
        ],
    )
    buckets, (to_a, to_b) = results[:lon_count], results[lon_count:]
    arrived = {0: buckets[0]}
    first, second = routes(lat_count, lon_count)
    pair = lambda k: [(i, i ^ k) for i in range(lon_count)]
    sends = {k: (buckets[k], "lon", pair(k)) for k in range(1, lon_count)}
    sends["a"] = (to_a, ("lon", "lat"), first)
    sends["b"] = (to_b, ("lon", "lat"), second)
    sequence, groups = PLAN(lon_count)
    for key, ahead in sequence:
        block, axes, pairs = sends[key]
        if ahead is not None:
            block, arrived[ahead] = lax.optimization_barrier((block, arrived[ahead]))
        arrived[key] = lax.ppermute(block, axes, pairs)
    shape = (channels, rows, columns)
    size_of = lambda group: [
        pltpu.VMEM(((channels + 1) * rows, 2 * len(group) * bound), BF16),
        pltpu.VMEM((columns, 2 * len(group) * bound), BF16),
    ]
    advected = call(
        lambda *refs: stencil_kernel(*refs, carriers=carriers),
        "stencil", f32(*shape), c, speed, land_mask, fold_map.reshape(1, columns),
        arrived["a"], arrived["b"], *[arrived[k] for k in carriers],
        cost=cost(1.5),
    )
    sums = []
    for group in groups[:-1]:
        sums = [
            call(
                lambda *refs: scatter_kernel(*refs, messages=len(group), bound=bound, shape=shape),
                "scatter",
                f32((channels + 1) * rows, columns),
                *[arrived[k] for k in group],
                *sums,
                scratch=size_of(group),
                cost=cost(len(group)),
            )
        ]
    group = groups[-1]
    after = call(
        lambda *refs: final_kernel(
            *refs, messages=len(group), bound=bound, shape=shape
        ),
        "final",
        f32(*shape),
        *[arrived[k] for k in group],
        *sums,
        advected,
        scratch=size_of(group) + [pltpu.VMEM(shape, F32), pltpu.SemaphoreType.DMA((len(CUTS) + 1,))],
        out_specs=HBM,
        cost=cost(len(group)),
    )
    return after.reshape(tracer.shape)


def solution(mesh):
    in_specs = (
        P(None, None, "lat", "lon"),
        P(None, None, "lat", "lon"),
        P("lat", "lon"),
        P("lon"),
        P(None, None, "lat", "lon"),
        P("lat", "lon"),
        P("lat", "lon"),
    )
    out_specs = P(None, None, "lat", "lon")
    return jax.shard_map(body, mesh=mesh, in_specs=in_specs, out_specs=out_specs, check_vma=False)
```

```python
import jax
import jax.numpy as jnp
from jax import lax
from jax.experimental import pallas as pl
from jax.experimental.pallas import tpu as pltpu
from jax.sharding import PartitionSpec as P

DIFFUSION = 0.15
LANES = 128
LIMIT = 32 << 20
SCALE = 1e9
DEPTH = 5
STEP = 8
F32 = jnp.float32
BF16 = jnp.bfloat16
NT = (((1,), (1,)), ((), ()))


def halves(x):
    high = x.astype(BF16).astype(F32)
    return high, x - high


def iota(shape, dim):
    return lax.broadcasted_iota(jnp.int32, shape, dim)


def prepare_kernel(*refs, count, bound, cells, carriers):
    sources, out_refs, edge_refs = refs[:6], refs[6 : 6 + count], refs[6 + count : 8 + count]
    held, (left_ref, hot_ref, sems) = refs[8 + count : 14 + count], refs[14 + count :]
    copies = [
        pltpu.make_async_copy(source, ref, sems.at[n])
        for n, (source, ref) in enumerate(zip(sources, held))
    ]
    for copy in copies:
        copy.start()
    copies[0].wait()
    parent_ref, volume_ref, field_ref, *grid_refs = held
    blocks = parent_ref.shape[0]
    channels = field_ref.shape[0] // blocks
    shift = cells.bit_length() - 1
    parent = parent_ref[...]
    me = lax.axis_index("lon")
    owner = lax.bitwise_xor(lax.shift_right_arithmetic(parent, shift), me)
    owner = jnp.where(parent >= 0, owner, -1)
    inside = (lax.bitwise_and(parent, cells - 1) + 1).astype(F32)
    member = jnp.concatenate([jnp.where(owner == d, 1.0, 0.0) for d in range(count)], axis=0)
    square = (LANES, LANES)
    before = jnp.where(iota(square, 0) < iota(square, 1), 1.0, 0.0).astype(BF16)
    within = jnp.dot(member.astype(BF16), before, preferred_element_type=F32)
    total = jnp.broadcast_to(jnp.sum(member, axis=1, keepdims=True), member.shape)
    rows = count * blocks
    one, two = iota((rows, rows), 0), iota((rows, rows), 1)
    bits = blocks.bit_length() - 1
    same = lax.shift_right_logical(one, bits) == lax.shift_right_logical(two, bits)
    earlier = jnp.where(same & (two < one), 1.0, 0.0).astype(BF16)
    place = within + jnp.dot(earlier, total.astype(BF16), preferred_element_type=F32)
    picked = place * member
    rank = picked[:blocks]
    for d in range(1, count):
        rank = rank + picked[d * blocks : (d + 1) * blocks]
    rank = jnp.where(parent >= 0, rank, -1.0).astype(jnp.int32)
    extra = count * 2 * channels
    copies[1].wait()
    copies[2].wait()
    for b in range(blocks):
        lanes = slice(b * LANES, (b + 1) * LANES)
        spots = iota((bound, LANES), 0)
        hot_ref[:, lanes] = jnp.where(spots == rank[b : b + 1], 1.0, 0.0).astype(BF16)
        volume = volume_ref[b : b + 1, :]
        mass = field_ref[pl.ds(b, channels, stride=blocks), :] * volume
        pair = jnp.concatenate(halves(mass), axis=0).astype(BF16)
        mine = [member[d * blocks + b : d * blocks + b + 1] for d in range(count)]
        for d in range(count):
            chosen = jnp.broadcast_to(mine[d], (16, LANES)).astype(BF16)
            chosen = jnp.concatenate([chosen] * (2 * channels // 16), axis=0)
            left_ref[d * 2 * channels : (d + 1) * 2 * channels, lanes] = pair * chosen
        mask = jnp.concatenate(mine, axis=0)
        small = [h * mask for x in (volume, inside[b : b + 1]) for h in halves(x)]
        left_ref[extra : extra + 4 * count, lanes] = jnp.concatenate(small, axis=0).astype(BF16)
    result = lax.dot_general(left_ref[...], hot_ref[...], NT, preferred_element_type=F32)
    pieces = bound // LANES
    volumes = result[extra : extra + count] + result[extra + count : extra + 2 * count]
    insides = (
        result[extra + 2 * count : extra + 3 * count] + result[extra + 3 * count : extra + 4 * count]
    )
    base = pieces * channels
    for d in range(count):
        top = d * 2 * channels
        mass = result[top : top + channels] + result[top + channels : top + 2 * channels]
        for k in range(pieces):
            lanes = slice(k * LANES, (k + 1) * LANES)
            out_refs[d][k * channels : (k + 1) * channels, :] = mass[:, lanes]
            out_refs[d][base + k : base + k + 1, :] = volumes[d : d + 1, lanes]
            out_refs[d][base + pieces + k : base + pieces + k + 1, :] = insides[d : d + 1, lanes]
    for copy in copies[3:]:
        copy.wait()
    pack_edges(*grid_refs, {k: out_refs[k] for k in carriers}, *edge_refs, count)


def pack_edges(tracer_ref, velocity_ref, mask_ref, message_refs, a_ref, b_ref, count):
    channels, rows, columns = tracer_ref.shape
    levels = velocity_ref.shape[0] // 2
    ocean = mask_ref[...].astype(F32)
    lane = iota((rows, LANES), 1)
    edges = []
    for at in (0, columns - 1):
        edge = slice(at, at + 1)
        packed = jnp.where(lane < 3 * channels, ocean[:, edge], 0.0)
        for n in range(levels):
            spot = (lane >= channels) & (lane < 2 * channels) & (lane % levels == n)
            packed = jnp.where(spot, velocity_ref[n, :, edge], packed)
        for n in range(channels):
            packed = jnp.where(lane == n, tracer_ref[n, :, edge], packed)
        edges.append(packed)
    me = lax.axis_index("lon")
    for k, ref in message_refs.items():
        is_west = lax.bitwise_xor(me, k) == (me + count - 1) % count
        ref[ref.shape[0] - rows :, :] = jnp.where(is_west, edges[0], edges[1])
    odd = lax.axis_index("lat") % 2 == 1
    for top, n, ref in ((0, channels, tracer_ref), (channels, levels, velocity_ref)):
        start = 0 if top == 0 else levels
        first = ref[start : start + n, 0, :]
        last = ref[start : start + n, rows - 1, :]
        a_ref[top : top + n, :] = jnp.where(odd, last, first)
        b_ref[top : top + n, :] = jnp.where(odd, first, last)
    first = jnp.broadcast_to(ocean[0:1], (8, columns))
    last = jnp.broadcast_to(ocean[rows - 1 : rows], (8, columns))
    top = channels + levels
    a_ref[top : top + 8, :] = jnp.where(odd, last, first)
    b_ref[top : top + 8, :] = jnp.where(odd, first, last)


def shifted(x, west, east, south, north):
    rows, columns = x.shape
    lane = iota((rows, LANES), 1)
    row = iota((rows, columns), 0)
    tiles = [x[:, at : at + LANES] for at in range(0, columns, LANES)]
    left = [pltpu.roll(t, LANES - 1, 1) for t in tiles] + [east]
    right = [west] + [pltpu.roll(t, 1, 1) for t in tiles]
    pairs = range(len(tiles))
    return (
        jnp.concatenate([jnp.where(lane > 0, right[i + 1], right[i]) for i in pairs], axis=1),
        jnp.concatenate([jnp.where(lane < LANES - 1, left[i], left[i + 1]) for i in pairs], axis=1),
        jnp.where(row > 0, pltpu.roll(x, 1, 0), south),
        jnp.where(row < rows - 1, pltpu.roll(x, rows - 1, 0), north),
    )


def stencil_kernel(
    tracer_ref, velocity_ref, mask_ref, fold_ref, a_ref, b_ref, *refs, carriers
):
    message_refs, out_ref = refs[:-1], refs[-1]
    channels, rows, columns = tracer_ref.shape
    levels = velocity_ref.shape[0] // 2
    lat = lax.axis_index("lat")
    lon = lax.axis_index("lon")
    odd = lat % 2 == 1
    at_top = lat == lax.axis_size("lat") - 1
    count = lax.axis_size("lon")
    edges = [ref[ref.shape[0] - rows :, :] for ref in message_refs]
    west, east = edges[0], edges[0]
    for k, edge in zip(carriers[1:], edges[1:]):
        partner = lax.bitwise_xor(lon, k)
        west = jnp.where(partner == (lon + count - 1) % count, edge, west)
        east = jnp.where(partner == (lon + 1) % count, edge, east)
    north = jnp.where(odd, a_ref[...], b_ref[...])
    south = jnp.where(odd, b_ref[...], a_ref[...])
    partner = fold_ref[...] - (count - 1 - lon) * columns
    pick = jnp.where(iota((columns, columns), 0) == partner, 1.0, 0.0).astype(BF16)
    high, rest = halves(north)
    parts = jnp.concatenate([high, *halves(rest)], axis=0).astype(BF16)
    folded = jnp.dot(parts, pick, preferred_element_type=F32)
    height = north.shape[0]
    folded = folded[:height] + folded[height : 2 * height] + folded[2 * height :]
    turn = jnp.where(iota(folded.shape, 0) // levels == channels // levels, -1.0, 1.0)
    north = jnp.where(at_top, folded * turn, north)

    def sides(x, lane, row):
        return shifted(
            x, west[:, lane : lane + 1], east[:, lane : lane + 1],
            south[row : row + 1], north[row : row + 1],
        )

    ocean = mask_ref[...].astype(F32)
    ocean_sides = sides(ocean, 2 * channels, channels + levels)
    opens = [ocean * side for side in ocean_sides]
    for level in range(levels):
        u = velocity_ref[level]
        v = velocity_ref[levels + level]
        u_w, u_e, _, _ = sides(u, channels + level, channels + level)
        _, _, v_s, v_n = sides(v, channels + level, channels + level)
        speeds = 0.25 * (u + u_w), 0.25 * (u + u_e), 0.25 * (v + v_s), 0.25 * (v + v_n)
        own, weights = 1.0, []
        for o, speed, sign in zip(opens, speeds, (1.0, -1.0, 1.0, -1.0)):
            near = o * (speed - sign * DIFFUSION)
            far = o * (speed + sign * DIFFUSION)
            own = own + sign * near
            weights.append(sign * far)
        for n in range(level, channels, levels):
            c = tracer_ref[n]
            total = own * c
            for weight, side in zip(weights, sides(c, n, n)):
                total = total + weight * side
            out_ref[n] = total


def expand(slot_refs, left_ref, hot_ref, *, bound, shape):
    channels, rows, columns = shape
    pieces = bound // LANES
    base = pieces * channels
    bits = columns.bit_length() - 1
    slots = len(slot_refs) * bound
    for j, slot_ref in enumerate(slot_refs):
        for k in range(pieces):
            at = (j * pieces + k) * LANES
            here = slice(at, at + LANES)
            there = slice(slots + at, slots + at + LANES)
            spot = slot_ref[base + pieces + k : base + pieces + k + 1, :].astype(jnp.int32) - 1
            spot_row = lax.shift_right_arithmetic(spot, bits)
            spot_column = lax.bitwise_and(spot, columns - 1)
            hot = jnp.where(iota((columns, LANES), 0) == spot_column, 1.0, 0.0).astype(BF16)
            hot_ref[:, here] = hot
            hot_ref[:, there] = hot
            in_row = jnp.where(iota((rows, LANES), 0) == spot_row, 1.0, 0.0).astype(BF16)
            mass = slot_ref[k * channels : (k + 1) * channels, :]
            volume = slot_ref[base + k : base + k + 1, :]
            for x, top, n in ((volume, 0, 1), (mass, 1, channels)):
                for part, to in zip(halves(x), (here, there)):
                    for i in range(n):
                        spread = jnp.broadcast_to(part[i : i + 1], (16, LANES)).astype(BF16)
                        spread = jnp.concatenate([spread] * (rows // 16), axis=0)
                        left_ref[(top + i) * rows : (top + i + 1) * rows, to] = spread * in_row


def scatter_kernel(*refs, messages, bound, shape):
    slot_refs, (*sum_refs, out_ref, left_ref, hot_ref) = refs[:messages], refs[messages:]
    expand(slot_refs, left_ref, hot_ref, bound=bound, shape=shape)
    new = lax.dot_general(left_ref[...], hot_ref[...], NT, preferred_element_type=F32)
    for ref in sum_refs:
        new = new + ref[...]
    out_ref[...] = new


def final_kernel(*refs, messages, bound, shape):
    channels, rows, columns = shape
    slot_refs, refs = refs[:messages], refs[messages:]
    sum_ref, advected_ref, out_ref, left_ref, hot_ref, held_ref, sems = refs
    expand(slot_refs, left_ref, hot_ref, bound=bound, shape=shape)
    mass = lax.dot_general(left_ref[...], hot_ref[...], NT, preferred_element_type=F32)
    mass = mass + sum_ref[...]
    scale = 1.0 / (1.0 + mass[:rows])
    copies = []
    for n in range(channels):
        held_ref[n] = (advected_ref[n] + mass[(n + 1) * rows : (n + 2) * rows]) * scale
        if (n + 1) % STEP == 0:
            done = slice(n + 1 - STEP, n + 1)
            copies.append(
                pltpu.make_async_copy(held_ref.at[done], out_ref.at[done], sems.at[len(copies)])
            )
            copies[-1].start()
    for copy in copies:
        copy.wait()


VMEM = pl.BlockSpec(memory_space=pltpu.VMEM)


HBM = pl.BlockSpec(memory_space=pltpu.MemorySpace.HBM)


def cost(microseconds):
    return pl.CostEstimate(flops=int(SCALE * microseconds), bytes_accessed=0, transcendentals=0)


def call(kernel, name, outs, *args, scratch=(), specs=None, out_specs=None, cost=None):
    single = not isinstance(outs, (list, tuple))
    return pl.pallas_call(
        kernel,
        out_shape=outs,
        in_specs=specs or [VMEM] * len(args),
        out_specs=out_specs or (VMEM if single else [VMEM] * len(outs)),
        scratch_shapes=list(scratch),
        compiler_params=pltpu.CompilerParams(vmem_limit_bytes=LIMIT),
        cost_estimate=cost,
        name=name,
    )(*args)


def PLAN(count):
    far = list(range(count // 2, count - 1))
    near = [k for k in range(1, count // 2) if k & (k + 1)]
    carriers = [k for k in range(1, count // 2) if not k & (k + 1)][::-1]
    keys = ["b", "a", count - 1, far[0], *carriers, *far[1:], *near]
    sequence = [(key, keys[n - DEPTH] if n >= DEPTH else None) for n, key in enumerate(keys)]
    cut = 4 + len(carriers)
    return sequence, [[0], keys[2:cut], keys[cut : cut + 1], keys[cut + 1 :]]


def routes(lat_count, lon_count):
    first, second = [], []
    for lon in range(lon_count):
        for lat in range(lat_count):
            here = lon * lat_count + lat
            second.append((here, lon * lat_count + (lat ^ 1)))
            if lat == lat_count - 1:
                first.append((here, (lon_count - 1 - lon) * lat_count + lat))
            elif lat > 0:
                first.append((here, lon * lat_count + ((lat + 1) ^ 1) - 1))
    return first, second


def body(
    tracer, velocity, land_mask, fold_map, nested_tracer_field, nested_cell_volume, nest_parent
):
    tracers, levels, rows, columns = tracer.shape
    channels = tracers * levels
    lon_count, lat_count = lax.axis_size("lon"), lax.axis_size("lat")
    slot_count = nest_parent.shape[1]
    bound = 2 * slot_count // lon_count
    blocks = slot_count // LANES
    pieces = bound // LANES
    f32 = lambda *shape: jax.ShapeDtypeStruct(shape, F32)
    size = pieces * (channels + 2)
    carriers = [k for k in range(1, lon_count) if k & (k + 1) == 0]
    heights = [size + rows if k in carriers else size for k in range(lon_count)]
    c = tracer.reshape(channels, rows, columns)
    speed = velocity.reshape(2 * levels, rows, columns)
    line = f32(channels + levels + 8, columns)
    inputs = (
        nest_parent.reshape(blocks, LANES),
        nested_cell_volume.reshape(blocks, LANES),
        nested_tracer_field.reshape(channels * blocks, LANES),
        c, speed, land_mask,
    )
    results = call(
        lambda *refs: prepare_kernel(
            *refs, count=lon_count, bound=bound, cells=rows * columns, carriers=carriers
        ),
        "prepare",
        [f32(height, LANES) for height in heights] + [line, line],
        *[pltpu.with_memory_space_constraint(x, pltpu.MemorySpace.HBM) for x in inputs],
        specs=[HBM] * len(inputs),
        scratch=[pltpu.VMEM(x.shape, x.dtype) for x in inputs]
        + [
            pltpu.VMEM((lon_count * (2 * channels + 4), slot_count), BF16),
            pltpu.VMEM((bound, slot_count), BF16),
            pltpu.SemaphoreType.DMA((len(inputs),)),
        ],
    )
    buckets, (to_a, to_b) = results[:lon_count], results[lon_count:]
    arrived = {0: buckets[0]}
    first, second = routes(lat_count, lon_count)
    pair = lambda k: [(i, i ^ k) for i in range(lon_count)]
    sends = {k: (buckets[k], "lon", pair(k)) for k in range(1, lon_count)}
    sends["a"] = (to_a, ("lon", "lat"), first)
    sends["b"] = (to_b, ("lon", "lat"), second)
    sequence, groups = PLAN(lon_count)
    for key, ahead in sequence:
        block, axes, pairs = sends[key]
        if ahead is not None:
            block, arrived[ahead] = lax.optimization_barrier((block, arrived[ahead]))
        arrived[key] = lax.ppermute(block, axes, pairs)
    shape = (channels, rows, columns)
    size_of = lambda group: [
        pltpu.VMEM(((channels + 1) * rows, 2 * len(group) * bound), BF16),
        pltpu.VMEM((columns, 2 * len(group) * bound), BF16),
    ]
    advected = call(
        lambda *refs: stencil_kernel(*refs, carriers=carriers),
        "stencil", f32(*shape), c, speed, land_mask, fold_map.reshape(1, columns),
        arrived["a"], arrived["b"], *[arrived[k] for k in carriers],
        cost=cost(1.5),
    )
    sums = []
    for group in groups[:-1]:
        sums = [
            call(
                lambda *refs: scatter_kernel(*refs, messages=len(group), bound=bound, shape=shape),
                "scatter",
                f32((channels + 1) * rows, columns),
                *[arrived[k] for k in group],
                *sums,
                scratch=size_of(group),
                cost=cost(len(group)),
            )
        ]
    group = groups[-1]
    after = call(
        lambda *refs: final_kernel(
            *refs, messages=len(group), bound=bound, shape=shape
        ),
        "final",
        f32(*shape),
        *[arrived[k] for k in group],
        *sums,
        advected,
        scratch=size_of(group) + [pltpu.VMEM(shape, F32), pltpu.SemaphoreType.DMA((channels // STEP,))],
        out_specs=HBM,
        cost=cost(len(group)),
    )
    return after.reshape(tracer.shape)


def solution(mesh):
    in_specs = (
        P(None, None, "lat", "lon"),
        P(None, None, "lat", "lon"),
        P("lat", "lon"),
        P("lon"),
        P(None, None, "lat", "lon"),
        P("lat", "lon"),
        P("lat", "lon"),
    )
    out_specs = P(None, None, "lat", "lon")
    return jax.shard_map(body, mesh=mesh, in_specs=in_specs, out_specs=out_specs, check_vma=False)
```
